128 devices in a mesh: seq: 8 (over y, core), mp: 4 (over x), enc: 4 (over z).
Axes of the slice: x: 4, y: 4, z: 4, core: 2. Of those that a mesh axis runs over, the one named last changes fastest.
Arguments:
- self_q: bfloat16 [4, 2048, 8192], P('enc', 'seq', 'mp'), may hold values from -128 to 128
- self_k: bfloat16 [4, 2048, 1024], P('enc', 'seq', 'mp'), may hold values from -4 to 4
- self_v: bfloat16 [4, 2048, 1024], P('enc', 'seq', 'mp'), may hold values from -6 to 6
- doc_ids: int32 [4, 2048], P('enc'), may hold values from 0 to 3, never falling along the last dimension, each value on 1 to 1024 neighbouring positions
- cross_q: bfloat16 [4, 2048, 8192], P('enc', 'seq', 'mp'), may hold values from -128 to 128
- image_keys: bfloat16 [128, 128, 1024], P(('seq', 'enc'), 'mp'), may hold values from -4 to 4
- image_values: bfloat16 [128, 128, 1024], P(('seq', 'enc'), 'mp'), may hold values from -6 to 6
- image_list: int32 [4, 8, 32], replicated, may hold values from 0 to 127, as said below
- image_lengths: int32 [128], replicated, may hold values from 32 to 128, as said below
- cross_mask: int32 [4, 16, 32], P('enc', 'seq'), may hold values from 0 to 1, as said below
Outputs:
- self_out: bfloat16 [4, 2048, 8192], P('enc', 'seq', 'mp')
- cross_out: bfloat16 [4, 2048, 8192], P('enc', 'seq', 'mp')
The draws below stay inside these ranges and needn't reach their ends.
Inputs may be any that keep to these rules, and one draw needn't show every extreme that they name: `image_list`: the 32 images of a block are distinct. Image i is held at index i // 4 of seq+enc (seq slowest). No block lists more than 2 images of one holder, and every block lists exactly 2 images of some holder. `image_lengths`: A whole number of tiles of 32 slots, one to four tiles; some image has all 128 slots live. `cross_mask`: the first 128 tokens of each sequence attend no image; every later mask block attends the image in its slot 0.
All inputs are finite; a program needn't handle non-finite values.
Results may differ from the reference program's by a relative error of at most 0.0047.
Values may be sent and summed in bfloat16 or wider, within the bound.
A program may use at most 128 MiB of HBM per device.

```python
import math
import jax
import jax.numpy as jnp
import numpy as np
from jax import lax

H = 64
KVH = 8
HD = 128
TOK_DEV = 256
XBLK = 128
TILE_TOK = 32
CAP = 2
IMG_DEV = 4
DOCS = 4
IMG_TOK = 128
SEQS = 4
BLOCKS = 8
HOLDERS = 32
MAXIMG = 32
TOKENS = 2048
IMAGES = 128


def clipped_normal(seed_key, full_shape):
    return jnp.clip(jax.random.normal(seed_key, full_shape, jnp.float32), -4.0, 4.0)


def self_key_rows(key):
    key_values = clipped_normal(jax.random.fold_in(key, 11), (SEQS, TOKENS, KVH * HD))
    return key_values


def image_key_rows(key):
    key_values = clipped_normal(jax.random.fold_in(key, 31), (IMAGES, IMG_TOK, KVH * HD))
    return key_values


def one_list(block_key):
    owner_key, count_key, local_key, order_key = jax.random.split(block_key, 4)
    owners = jax.random.permutation(owner_key, HOLDERS)
    paired_count = jax.random.randint(count_key, (), max(1, MAXIMG - HOLDERS), MAXIMG // CAP + 1)
    local_orders = jax.vmap(lambda sub_key: jax.random.permutation(sub_key, IMG_DEV))(jax.random.split(local_key, HOLDERS))
    position = jnp.arange(MAXIMG)
    in_pair = position < CAP * paired_count
    owner_slot = jnp.where(in_pair, position // CAP, paired_count + position - CAP * paired_count)
    within = jnp.where(in_pair, position % CAP, 0)
    holder = owners[owner_slot]
    images = holder * IMG_DEV + local_orders[holder, within]
    return images[jax.random.permutation(order_key, MAXIMG)].astype(jnp.int32)


def list_table(key):
    block_keys = jax.random.split(jax.random.fold_in(key, 51), SEQS * BLOCKS)
    return jax.vmap(one_list)(block_keys).reshape(SEQS, BLOCKS, MAXIMG)


def draw_self_k(key, part):
    return self_key_rows(key).astype(jnp.bfloat16)


def draw_self_q(key, part):
    full_shape = (SEQS, TOKENS, H * HD)
    result = jnp.clip(jax.random.normal(jax.random.fold_in(key, 22), full_shape, jnp.float32), -6.0, 6.0)
    return result.astype(jnp.bfloat16)


def draw_image_keys(key, part):
    return image_key_rows(key).astype(jnp.bfloat16)


def draw_cross_q(key, part):
    full_shape = (SEQS, TOKENS, H * HD)
    result = jnp.clip(jax.random.normal(jax.random.fold_in(key, 43), full_shape, jnp.float32), -6.0, 6.0)
    return result.astype(jnp.bfloat16)


def draw_image_list(key, part):
    return list_table(key)


def draw_image_lengths(key, part):
    tiles = jax.random.randint(jax.random.fold_in(key, 61), (IMAGES,), 1, 5)
    fullest = jax.random.randint(jax.random.fold_in(key, 62), (), 0, IMAGES)
    tiles = tiles.at[fullest].set(4)
    return (tiles * TILE_TOK).astype(jnp.int32)


def draw_cross_mask(key, part):
    flags = jax.random.randint(jax.random.fold_in(key, 71), (SEQS, TOKENS // XBLK, MAXIMG), 0, 3)
    flags = (flags > 0).astype(jnp.int32)
    flags = flags.at[:, :, 0].set(1)
    flags = flags.at[:, 0, :].set(0)
    return flags


def level_of(key, extent, cuts, low, high):
    def one(axis_at, blocks):
        draws = jax.random.uniform(jax.random.fold_in(jax.random.fold_in(key, 6), axis_at), (blocks,), jnp.float32, low / len(cuts), high / len(cuts))
        return jnp.repeat(jnp.exp(draws), extent[axis_at] // blocks).reshape((-1,) + (1,) * (len(extent) - axis_at - 1))

    loudness = one(*cuts[0])
    for cut in cuts[1:]:
        loudness = loudness * one(*cut)
    return loudness


def length_profile(amount, total, reach, lean):
    portions = [(1 << 20) // math.isqrt(standing ** lean) + 1 for standing in range(2, amount + 1)]
    rest, counts = total - reach - (amount - 1), [1] * (amount - 1)
    while rest > 0:
        free = [i for i in range(amount - 1) if counts[i] < reach]
        whole, left = sum([portions[i] for i in free]), rest
        for i in free:
            more = min(reach - counts[i], max(1, left * portions[i] // whole), rest)
            counts[i] = counts[i] + more
            rest = rest - more
    return np.array([reach] + counts)


def uneven(own_key, amount, total, bound, lean):
    if amount == 2:
        one = jax.random.randint(own_key, (), max(1, total - bound), min(bound, total - 1) + 1)
        return jnp.stack([one, total - one])
    sizes = jnp.asarray(length_profile(amount, total, bound, lean), jnp.int32)
    pairs = (amount - 1) // 2
    source_of, receiver = sizes[1:1 + 2 * pairs:2], sizes[2:2 + 2 * pairs:2]
    slack = jnp.minimum(source_of - 1, bound - receiver)
    moved = jax.random.randint(jax.random.fold_in(own_key, 1), (pairs,), 0, 1 << 20) % (slack + 1)
    sizes = sizes.at[1:1 + 2 * pairs:2].set(source_of - moved).at[2:2 + 2 * pairs:2].set(receiver + moved)
    return sizes[jax.random.permutation(jax.random.fold_in(own_key, 2), amount)]


def noise(key, dims, scale, limit, cuts=(), held_as=jnp.bfloat16):
    values = jax.random.normal(key, dims, jnp.float32) * scale
    if len(cuts) > 0:
        values = level_of(key, dims, cuts, -0.22, 0.18) * values
    return jnp.clip(values, min=-limit, max=limit).astype(held_as)


def setup_inputs(seed: int = 0) -> dict:
    arg_keys = jax.random.split(jax.random.key(seed), 11)
    self_q = draw_self_q(jax.random.fold_in(arg_keys[10], 71), 0)
    self_k = draw_self_k(jax.random.fold_in(arg_keys[10], 71), 0)
    self_v = noise(arg_keys[2], (SEQS, TOKENS, KVH * HD), 1.0, 6.0, ((0, 4), (1, 8), (2, 4)))
    doc_ids = jax.vmap(lambda own: jnp.searchsorted(jnp.cumsum(uneven(own, DOCS, TOKENS, TOKENS // 2, 0)), jnp.arange(TOKENS), side="right"))(jax.random.split(arg_keys[3], SEQS)).reshape((SEQS, TOKENS)).astype(jnp.int32)
    cross_q = draw_cross_q(jax.random.fold_in(arg_keys[10], 71), 0)
    image_keys = draw_image_keys(jax.random.fold_in(arg_keys[10], 71), 0)
    image_values = noise(arg_keys[6], (IMAGES, IMG_TOK, KVH * HD), 1.0, 6.0, ((0, 32), (1, 4)))
    image_list = draw_image_list(jax.random.fold_in(arg_keys[10], 71), 0)
    image_lengths = draw_image_lengths(jax.random.fold_in(arg_keys[10], 71), 0)
    cross_mask = draw_cross_mask(jax.random.fold_in(arg_keys[10], 71), 0)
    return dict(self_q=self_q, self_k=self_k, self_v=self_v, doc_ids=doc_ids, cross_q=cross_q, image_keys=image_keys, image_values=image_values, image_list=image_list, image_lengths=image_lengths, cross_mask=cross_mask)


NEG_FILL = -1e30


def masked_attend(queries, keys, values, allowed, scale_factor):
    scores = jnp.einsum("rkgd,skd->rkgs", queries.astype(jnp.float32), keys.astype(jnp.float32)) * scale_factor
    wide_mask = allowed[:, None, None, :]
    scores = jnp.where(wide_mask, scores, NEG_FILL)
    row_top = jnp.max(scores, axis=-1, keepdims=True)
    row_top = jnp.where(row_top > -1e29, row_top, 0.0)
    weights = jnp.where(wide_mask, jnp.exp(scores - row_top), 0.0)
    totals = jnp.sum(weights, axis=-1, keepdims=True)
    low_weights = lax.optimization_barrier(weights.astype(jnp.bfloat16)).astype(jnp.float32)
    mixed = jnp.einsum("rkgs,skd->rkgd", low_weights, values.astype(jnp.float32))
    return (mixed / jnp.maximum(totals, 1.0)).astype(jnp.bfloat16)


def reference(self_q, self_k, self_v, doc_ids, cross_q, image_keys, image_values, image_list, image_lengths, cross_mask):
    group_size = H // KVH
    scale_factor = HD ** -0.5
    seq_count = self_q.shape[0]
    seq_tokens = self_q.shape[1]
    row_block = min(128, seq_tokens)
    block_count = seq_tokens // row_block
    positions = jnp.arange(seq_tokens, dtype=jnp.int32)
    zero_index = jnp.zeros((), jnp.int32)

    def self_rows(flat_number):
        seq_number = (flat_number // block_count).astype(jnp.int32)
        row_start = ((flat_number % block_count) * row_block).astype(jnp.int32)
        queries = lax.dynamic_slice(self_q, (seq_number, row_start, zero_index), (1, row_block, H * HD))[0]
        queries = queries.reshape(row_block, KVH, group_size, HD)
        keys = lax.dynamic_index_in_dim(self_k, seq_number, 0, keepdims=False).reshape(seq_tokens, KVH, HD)
        values = lax.dynamic_index_in_dim(self_v, seq_number, 0, keepdims=False).reshape(seq_tokens, KVH, HD)
        documents = lax.dynamic_index_in_dim(doc_ids, seq_number, 0, keepdims=False)
        row_docs = lax.dynamic_slice_in_dim(documents, row_start, row_block, 0)
        row_positions = row_start + jnp.arange(row_block, dtype=jnp.int32)
        allowed = (row_docs[:, None] == documents[None, :]) & (positions[None, :] <= row_positions[:, None])
        return masked_attend(queries, keys, values, allowed, scale_factor).reshape(row_block, H * HD)

    self_flat = lax.map(self_rows, jnp.arange(seq_count * block_count, dtype=jnp.int32))
    self_out = self_flat.reshape(seq_count, seq_tokens, H * HD)

    mask_blocks = seq_tokens // XBLK
    image_slots = image_keys.shape[1]
    slot_iota = jnp.arange(image_slots, dtype=jnp.int32)

    def cross_rows(flat_number):
        seq_number = (flat_number // mask_blocks).astype(jnp.int32)
        mask_number = (flat_number % mask_blocks).astype(jnp.int32)
        row_start = (mask_number * XBLK).astype(jnp.int32)
        text_block = (row_start // TOK_DEV).astype(jnp.int32)
        listed = image_list[seq_number, text_block]
        keys = image_keys[listed].reshape(MAXIMG * image_slots, KVH, HD)
        values = image_values[listed].reshape(MAXIMG * image_slots, KVH, HD)
        live = slot_iota[None, :] < image_lengths[listed][:, None]
        flags = cross_mask[seq_number, mask_number]
        allowed = ((flags[:, None] == 1) & live).reshape(1, MAXIMG * image_slots)
        allowed = jnp.broadcast_to(allowed, (XBLK, MAXIMG * image_slots))
        queries = lax.dynamic_slice(cross_q, (seq_number, row_start, zero_index), (1, XBLK, H * HD))[0]
        queries = queries.reshape(XBLK, KVH, group_size, HD)
        return masked_attend(queries, keys, values, allowed, scale_factor).reshape(XBLK, H * HD)

    cross_flat = lax.map(cross_rows, jnp.arange(seq_count * mask_blocks, dtype=jnp.int32))
    cross_out = cross_flat.reshape(seq_count, seq_tokens, H * HD)
    return self_out, cross_out
```

```python
import functools
import jax
import jax.numpy as jnp
from jax import lax
from jax.experimental import pallas as pl
from jax.experimental.pallas import tpu as pltpu
from jax.sharding import PartitionSpec as P

HD = 128
NEG = -1e30
LOG2E = 1.4426950408889634
FACTOR = HD ** (-0.5) * LOG2E
MESH = pl.DeviceIdType.MESH
TILE = 32
CHUNK = 512
NT = (((1,), (1,)), ((), ()))


def exchange(ik, iv, sk, sv, kv, skv, mp_s, mp_r, own_s, r1_s, r1_r, r2_s, r2_r, sib_s, sib_r, tx_s, tx_r):
    s = lax.axis_index("seq")
    g = lax.axis_index("mp")
    e = lax.axis_index("enc")
    core = lax.rem(s, 2)
    y = s // 2
    sibling = s + 1 - 2 * core
    me = s * 4 + e
    p1 = e + core * (y - e)
    p2 = y + core * (e - y)

    def at(q1, q2):
        yy = q2 + core * (q1 - q2)
        zz = q1 + core * (q2 - q1)
        return (2 * yy + core, g, zz)

    def holder(q1, q2):
        return (1 + 7 * core) * q1 + (8 - 7 * core) * q2 + 4 * core

    up = lambda p: lax.rem(p + 1, 4)
    down = lambda p: lax.rem(p + 3, 4)

    barrier = pltpu.get_barrier_semaphore()
    greet = [at(up(p1), p2), at(down(p1), p2), at(p1, up(p2)), at(p1, down(p2)), (sibling, g, e)]
    greet += [(s, lax.rem(g + d, 4), e) for d in (1, 2, 3)]
    for who in greet:
        pl.semaphore_signal(barrier, inc=1, device_id=who, device_id_type=MESH)
    pl.semaphore_wait(barrier, len(greet))

    def remote(src, dst, ss, rs, who):
        return pltpu.make_async_remote_copy(
            src_ref=src, dst_ref=dst, send_sem=ss, recv_sem=rs, device_id=who, device_id_type=MESH
        )

    mine = pl.ds(pl.multiple_of(g * TILE, TILE), TILE)
    first = []
    for d in (1, 2, 3):
        to = lax.rem(g + d, 4)
        cols = pl.ds(pl.multiple_of(to * 256, 256), 256)
        for half, src in ((0, ik), (1, iv)):
            c = remote(
                src.at[:, :, cols], kv.at[me, half, :, mine, :],
                mp_s.at[d - 1, half], mp_r.at[d - 1, half], (s, to, e),
            )
            c.start()
            first.append(c)
    cols = pl.ds(pl.multiple_of(g * 256, 256), 256)
    for half, src in ((0, ik), (1, iv)):
        c = pltpu.make_async_copy(src.at[:, :, cols], kv.at[me, half, :, mine, :], own_s.at[half])
        c.start()
        first.append(c)

    text = []

    def guarded(cond, c):
        text.append((cond, c))

        @pl.when(cond)
        def _():
            c.start()

    for half, src in ((0, sk), (1, sv)):
        guarded(s + 2 < 8, remote(src, skv.at[1, half], tx_s.at[0, half], tx_r.at[0, half], (lax.rem(s + 2, 8), g, e)))
        guarded(core == 0, remote(src, skv.at[0, half], tx_s.at[1, half], tx_r.at[1, half], (sibling, g, e)))

    for c in first:
        c.wait()

    sends = []

    def piece(i1, i2):
        q1 = (p1, down(p1), up(p1), lax.rem(p1 + 2, 4))[i1]
        q2 = (p2, down(p2), up(p2), lax.rem(p2 + 2, 4))[i2]
        return holder(q1, q2)

    def go(h, half, ss, rs, who):
        c = remote(kv.at[h, half], kv.at[h, half], ss, rs, who)
        c.start()
        sends.append(c)

    def landed(h, half, rs):
        pltpu.make_async_copy(kv.at[h, half], kv.at[h, half], rs).wait()

    right1, left1 = at(up(p1), p2), at(down(p1), p2)
    right2, left2 = at(p1, up(p2)), at(p1, down(p2))

    def to_sibling(i1, i2, half):
        go(piece(i1, i2), half, sib_s.at[i1, i2, half], sib_r.at[i1, i2, half], (sibling, g, e))

    def ring2(i1, half):
        h = piece(i1, 0)
        go(h, half, r2_s.at[i1, 0, half], r2_r.at[i1, 0, half], right2)
        go(h, half, r2_s.at[i1, 1, half], r2_r.at[i1, 1, half], left2)

    for half in (0, 1):
        h = piece(0, 0)
        go(h, half, r1_s.at[0, half], r1_r.at[0, half], right1)
        go(h, half, r1_s.at[1, half], r1_r.at[1, half], left1)
    for half in (0, 1):
        ring2(0, half)
    for half in (0, 1):
        to_sibling(0, 0, half)

    landed(piece(1, 0), 0, r1_r.at[0, 0])
    go(piece(1, 0), 0, r1_s.at[2, 0], r1_r.at[2, 0], right1)
    landed(piece(2, 0), 0, r1_r.at[1, 0])
    landed(piece(1, 0), 1, r1_r.at[0, 1])
    landed(piece(2, 0), 1, r1_r.at[1, 1])
    go(piece(2, 0), 1, r1_s.at[2, 1], r1_r.at[2, 1], left1)
    for i1 in (1, 2):
        for half in (0, 1):
            ring2(i1, half)

    def text_landed(cond, slot, half, sem):
        @pl.when(cond)
        def _():
            pltpu.make_async_copy(skv.at[slot, half], skv.at[slot, half], sem).wait()

    for half in (0, 1):
        text_landed(s >= 2, 1, half, tx_r.at[0, half])
        text_landed(core == 1, 0, half, tx_r.at[1, half])
        got = skv.at[1, half]
        guarded((s >= 2) & (core == 0), remote(got, skv.at[2, half], tx_s.at[2, half], tx_r.at[2, half], (sibling, g, e)))
        guarded((s >= 2) & (core == 1), remote(got, skv.at[0, half], tx_s.at[3, half], tx_r.at[3, half], (sibling, g, e)))
        guarded((s >= 2) & (s + 2 < 8), remote(got, skv.at[3, half], tx_s.at[4, half], tx_r.at[4, half], (lax.rem(s + 2, 8), g, e)))

    for half in (0, 1):
        landed(piece(3, 0), half, r1_r.at[2, half])
        ring2(3, half)
    for i1 in (1, 2, 3):
        for half in (0, 1):
            to_sibling(i1, 0, half)

    for i1 in (0, 1, 2, 3):
        landed(piece(i1, 1), 0, r2_r.at[i1, 0, 0])
        go(piece(i1, 1), 0, r2_s.at[i1, 2, 0], r2_r.at[i1, 2, 0], right2)
        to_sibling(i1, 1, 0)
        landed(piece(i1, 2), 0, r2_r.at[i1, 1, 0])
        to_sibling(i1, 2, 0)
        landed(piece(i1, 1), 1, r2_r.at[i1, 0, 1])
        to_sibling(i1, 1, 1)
        landed(piece(i1, 2), 1, r2_r.at[i1, 1, 1])
        go(piece(i1, 2), 1, r2_s.at[i1, 2, 1], r2_r.at[i1, 2, 1], left2)
        to_sibling(i1, 2, 1)
        if i1 == 1:
            for half in (0, 1):
                text_landed((s >= 2) & (core == 1), 2, half, tx_r.at[2, half])
                text_landed((s >= 2) & (core == 0), 0, half, tx_r.at[3, half])
                text_landed(s >= 4, 3, half, tx_r.at[4, half])
                got = skv.at[3, half]
                guarded((s >= 4) & (core == 1), remote(got, skv.at[2, half], tx_s.at[5, half], tx_r.at[5, half], (sibling, g, e)))
    for i1 in (0, 1, 2, 3):
        for half in (0, 1):
            landed(piece(i1, 3), half, r2_r.at[i1, 2, half])
            to_sibling(i1, 3, half)
    for half in (0, 1):
        text_landed((s >= 4) & (core == 0), 2, half, tx_r.at[5, half])

    other = 1 - core
    o1 = e + other * (y - e)
    o2 = y + other * (e - y)
    for i1 in range(4):
        for i2 in range(4):
            q1 = (o1, down(o1), up(o1), lax.rem(o1 + 2, 4))[i1]
            q2 = (o2, down(o2), up(o2), lax.rem(o2 + 2, 4))[i2]
            h = (1 + 7 * other) * q1 + (8 - 7 * other) * q2 + 4 * other
            for half in (0, 1):
                landed(h, half, sib_r.at[i1, i2, half])
    for c in sends:
        c.wait_send()
    for cond, c in text:
        @pl.when(cond)
        def _():
            c.wait_send()


def softmax_step(sc, m_ref, l_ref, a_ref, v, idx):
    m_old = m_ref[idx]
    top = jnp.max(sc, axis=1, keepdims=True)
    m_new = jnp.maximum(m_old, top)
    p = jnp.exp2((sc - m_new[:, :1]) * FACTOR)
    alpha = jnp.exp2((m_old - m_new) * FACTOR)
    part = p[:, 0:128]
    for i in range(1, sc.shape[1] // 128):
        part = part + p[:, i * 128:(i + 1) * 128]
    l_ref[idx] = l_ref[idx] * alpha + part
    a_ref[idx] = a_ref[idx] * alpha + jnp.dot(p.astype(jnp.bfloat16), v, preferred_element_type=jnp.float32)
    m_ref[idx] = m_new


def finish(l_ref, a_ref, idx):
    total = jnp.sum(l_ref[idx], axis=1, keepdims=True)
    return (a_ref[idx] / jnp.maximum(total, 1.0)).astype(jnp.bfloat16)


def self_kernel(doc_ref, q_ref, k_ref, v_ref, skv_ref, out_ref, bias, m_ref, l_ref, a_ref):
    s = lax.axis_index("seq")
    half_rows = 128

    def row_docs(block):
        return doc_ref[:, pl.ds(pl.multiple_of(block * 256, 256), 256)].astype(jnp.float32)

    own = row_docs(s)
    down = jnp.concatenate(
        [jnp.transpose(jnp.broadcast_to(own[:, i * 128:(i + 1) * 128], (128, 128))) for i in (0, 1)], axis=0
    )
    down = jnp.concatenate([down, down], axis=1)
    rows = lax.broadcasted_iota(jnp.int32, (256, 256), 0)
    cols = lax.broadcasted_iota(jnp.int32, (256, 256), 1)
    bias[0] = jnp.where((down == own) & (cols <= rows), 0.0, NEG)
    for d in range(1, 5):
        @pl.when(s >= d)
        def _():
            bias[d] = jnp.where(down == row_docs(s - d), 0.0, NEG)

    for j in range(2):
        kcols = slice(j * 128, (j + 1) * 128)
        m_ref[...] = jnp.full_like(m_ref, NEG)
        l_ref[...] = jnp.zeros_like(l_ref)
        a_ref[...] = jnp.zeros_like(a_ref)
        for d in range(5):
            @pl.when(s >= d)
            def _():
                if d == 0:
                    k, v = k_ref[:, kcols], v_ref[:, kcols]
                else:
                    k, v = skv_ref[d - 1, 0, :, kcols], skv_ref[d - 1, 1, :, kcols]

                @pl.loop(0, 8)
                def _(h):
                    hc = pl.ds(pl.multiple_of((j * 8 + h) * 128, 128), 128)
                    for r in range(2):
                        rr = slice(r * half_rows, (r + 1) * half_rows)
                        sc = lax.dot_general(q_ref[rr, hc], k, NT, preferred_element_type=jnp.float32)
                        softmax_step(sc + bias[d, rr, :], m_ref, l_ref, a_ref, v, 2 * h + r)
        @pl.loop(0, 8)
        def _(h):
            hc = pl.ds(pl.multiple_of((j * 8 + h) * 128, 128), 128)
            for r in range(2):
                out_ref[r * half_rows:(r + 1) * half_rows, hc] = finish(l_ref, a_ref, 2 * h + r)


def cross_kernel(list_ref, len_ref, mask_ref, q_ref, kv_ref, out_ref, kbuf, vbuf, m_ref, l_ref, a_ref, ksem, vsem):
    s = lax.axis_index("seq")
    e = lax.axis_index("enc")
    per = CHUNK // TILE

    def tile_copies(r, img, t, pos):
        rows = pl.ds(pl.multiple_of(t * TILE, TILE), TILE)
        to = pl.ds(pl.multiple_of(pos * TILE, TILE), TILE)
        chunk = pos // per
        for half, buf, sem in ((0, kbuf, ksem), (1, vbuf, vsem)):
            pltpu.make_async_copy(
                kv_ref.at[img // 4, half, lax.rem(img, 4), rows, :], buf.at[r, to, :], sem.at[r, chunk]
            ).start()

    counts = []
    for r in range(2):
        def slot(k, pos):
            img = list_ref[e, s, k]
            n = jnp.where(mask_ref[0, r, k] == 1, len_ref[img] // TILE, 0)

            def one(t, p):
                tile_copies(r, img, t, p)
                return p + 1

            return lax.fori_loop(0, n, one, pos)

        n = lax.fori_loop(0, 32, slot, 0)
        chunks = (n + per - 1) // per

        def pad(p, c):
            tile_copies(r, list_ref[e, s, 0], 0, p)
            return c

        lax.fori_loop(n, chunks * per, pad, 0)
        counts.append((n, chunks))

    for r in range(2):
        n, chunks = counts[r]
        rr = slice(r * 128, (r + 1) * 128)
        m_ref[...] = jnp.full_like(m_ref, NEG)
        l_ref[...] = jnp.zeros_like(l_ref)
        a_ref[...] = jnp.zeros_like(a_ref)

        def chunk(c, carry):
            at = pl.ds(pl.multiple_of(c * CHUNK, CHUNK), CHUNK)
            for buf, sem in ((kbuf, ksem), (vbuf, vsem)):
                pltpu.make_async_copy(buf.at[r, at, :], buf.at[r, at, :], sem.at[r, c]).wait()
            keys = lax.broadcasted_iota(jnp.int32, (128, CHUNK), 1)
            dead = keys >= n * TILE - c * CHUNK
            for j in range(2):
                kcols = slice(j * 128, (j + 1) * 128)
                for h in range(8):
                    i = j * 8 + h
                    sc = lax.dot_general(
                        q_ref[rr, i * 128:(i + 1) * 128], kbuf[r, at, kcols], NT, preferred_element_type=jnp.float32
                    )
                    sc = jnp.where(dead, NEG, sc)
                    softmax_step(sc, m_ref, l_ref, a_ref, vbuf[r, at, kcols], i)
            return carry

        lax.fori_loop(0, chunks, chunk, 0)
        for i in range(16):
            out_ref[rr, i * 128:(i + 1) * 128] = finish(l_ref, a_ref, i)


def local(self_q, self_k, self_v, doc_ids, cross_q, image_keys, image_values, image_list, image_lengths, cross_mask):
    bf16 = jnp.bfloat16
    hbm = pl.BlockSpec(memory_space=pl.ANY)
    vm = pl.BlockSpec(memory_space=pltpu.VMEM)
    sm = pl.BlockSpec(memory_space=pltpu.SMEM)
    dma = lambda *shape: pltpu.SemaphoreType.DMA(shape)
    f32 = jnp.float32
    kv, skv = pl.pallas_call(
        exchange,
        name="exchange",
        out_shape=(
            jax.ShapeDtypeStruct((32, 2, 4, 128, 256), bf16),
            jax.ShapeDtypeStruct((4, 2, 256, 256), bf16),
        ),
        in_specs=[hbm] * 4,
        out_specs=(hbm, hbm),
        scratch_shapes=[
            dma(3, 2), dma(3, 2), dma(2), dma(3, 2), dma(3, 2), dma(4, 3, 2), dma(4, 3, 2),
            dma(4, 4, 2), dma(4, 4, 2), dma(6, 2), dma(6, 2),
        ],
        compiler_params=pltpu.CompilerParams(collective_id=0, has_side_effects=True),
    )(image_keys, image_values, self_k[0], self_v[0])
    self_out = pl.pallas_call(
        self_kernel,
        name="self_attend",
        out_shape=jax.ShapeDtypeStruct((256, 2048), bf16),
        in_specs=[vm] * 5,
        out_specs=vm,
        scratch_shapes=[
            pltpu.VMEM((5, 256, 256), f32), pltpu.VMEM((16, 128, 128), f32),
            pltpu.VMEM((16, 128, 128), f32), pltpu.VMEM((16, 128, 128), f32),
        ],
        compiler_params=pltpu.CompilerParams(vmem_limit_bytes=40 << 20),
    )(doc_ids, self_q[0], self_k[0], self_v[0], skv)
    cross_out = pl.pallas_call(
        cross_kernel,
        name="cross_attend",
        out_shape=jax.ShapeDtypeStruct((256, 2048), bf16),
        in_specs=[sm, sm, sm, vm, hbm],
        out_specs=vm,
        scratch_shapes=[
            pltpu.VMEM((2, 4096, 256), bf16), pltpu.VMEM((2, 4096, 256), bf16),
            pltpu.VMEM((16, 128, 128), f32), pltpu.VMEM((16, 128, 128), f32), pltpu.VMEM((16, 128, 128), f32),
            dma(2, 4096 // CHUNK), dma(2, 4096 // CHUNK),
        ],
        compiler_params=pltpu.CompilerParams(vmem_limit_bytes=40 << 20),
    )(image_list, image_lengths, cross_mask, cross_q[0], kv)
    return self_out[None], cross_out[None]


def solution(mesh):
    in_specs = (
        P("enc", "seq", "mp"),
        P("enc", "seq", "mp"),
        P("enc", "seq", "mp"),
        P("enc", None),
        P("enc", "seq", "mp"),
        P(("seq", "enc"), "mp", None),
        P(("seq", "enc"), "mp", None),
        P(),
        P(),
        P("enc", "seq", None),
    )
    out_specs = (P("enc", "seq", "mp"), P("enc", "seq", "mp"))
    return jax.shard_map(local, mesh=mesh, in_specs=in_specs, out_specs=out_specs, check_vma=False)
```

```python
import functools
import jax
import jax.numpy as jnp
from jax import lax
from jax.experimental import pallas as pl
from jax.experimental.pallas import tpu as pltpu
from jax.sharding import PartitionSpec as P

HD = 128
NEG = -1e30
LOG2E = 1.4426950408889634
FACTOR = HD ** (-0.5) * LOG2E
MESH = pl.DeviceIdType.MESH
TILE = 32
CHUNK = 512
NT = (((1,), (1,)), ((), ()))


def exchange(ik, iv, sk, sv, kv, skv, mp_s, mp_r, own_s, r1_s, r1_r, r2_s, r2_r, sib_s, sib_r, tx_s, tx_r):
    s = lax.axis_index("seq")
    g = lax.axis_index("mp")
    e = lax.axis_index("enc")
    core = lax.rem(s, 2)
    y = s // 2
    sibling = s + 1 - 2 * core
    me = s * 4 + e
    p1 = e + core * (y - e)
    p2 = y + core * (e - y)

    def at(q1, q2):
        yy = q2 + core * (q1 - q2)
        zz = q1 + core * (q2 - q1)
        return (2 * yy + core, g, zz)

    def holder(q1, q2):
        return (1 + 7 * core) * q1 + (8 - 7 * core) * q2 + 4 * core

    up = lambda p: lax.rem(p + 1, 4)
    down = lambda p: lax.rem(p + 3, 4)

    barrier = pltpu.get_barrier_semaphore()
    greet = [at(up(p1), p2), at(down(p1), p2), at(p1, up(p2)), at(p1, down(p2)), (sibling, g, e)]
    greet += [(s, lax.rem(g + d, 4), e) for d in (1, 2, 3)]
    for who in greet:
        pl.semaphore_signal(barrier, inc=1, device_id=who, device_id_type=MESH)
    pl.semaphore_wait(barrier, len(greet))

    def remote(src, dst, ss, rs, who):
        return pltpu.make_async_remote_copy(
            src_ref=src, dst_ref=dst, send_sem=ss, recv_sem=rs, device_id=who, device_id_type=MESH
        )

    mine = pl.ds(pl.multiple_of(g * TILE, TILE), TILE)
    first = []
    for d in (1, 2, 3):
        to = lax.rem(g + d, 4)
        cols = pl.ds(pl.multiple_of(to * 256, 256), 256)
        for half, src in ((0, ik), (1, iv)):
            c = remote(
                src.at[:, :, cols], kv.at[me, half, :, mine, :],
                mp_s.at[d - 1, half], mp_r.at[d - 1, half], (s, to, e),
            )
            c.start()
            first.append(c)
    cols = pl.ds(pl.multiple_of(g * 256, 256), 256)
    for half, src in ((0, ik), (1, iv)):
        c = pltpu.make_async_copy(src.at[:, :, cols], kv.at[me, half, :, mine, :], own_s.at[half])
        c.start()
        first.append(c)

    text = []

    def guarded(cond, c):
        text.append((cond, c))

        @pl.when(cond)
        def _():
            c.start()

    for half, src in ((0, sk), (1, sv)):
        guarded(s + 2 < 8, remote(src, skv.at[1, half], tx_s.at[0, half], tx_r.at[0, half], (lax.rem(s + 2, 8), g, e)))
        guarded(core == 0, remote(src, skv.at[0, half], tx_s.at[1, half], tx_r.at[1, half], (sibling, g, e)))

    for c in first:
        c.wait()

    sends = []

    def piece(i1, i2):
        q1 = (p1, down(p1), up(p1), lax.rem(p1 + 2, 4))[i1]
        q2 = (p2, down(p2), up(p2), lax.rem(p2 + 2, 4))[i2]
        return holder(q1, q2)

    def go(h, half, ss, rs, who):
        c = remote(kv.at[h, half], kv.at[h, half], ss, rs, who)
        c.start()
        sends.append(c)

    def landed(h, half, rs):
        pltpu.make_async_copy(kv.at[h, half], kv.at[h, half], rs).wait()

    right1, left1 = at(up(p1), p2), at(down(p1), p2)
    right2, left2 = at(p1, up(p2)), at(p1, down(p2))

    def to_sibling(i1, i2, half):
        go(piece(i1, i2), half, sib_s.at[i1, i2, half], sib_r.at[i1, i2, half], (sibling, g, e))

    def ring2(i1, half):
        h = piece(i1, 0)
        go(h, half, r2_s.at[i1, 0, half], r2_r.at[i1, 0, half], right2)
        go(h, half, r2_s.at[i1, 1, half], r2_r.at[i1, 1, half], left2)

    for half in (0, 1):
        h = piece(0, 0)
        go(h, half, r1_s.at[0, half], r1_r.at[0, half], right1)
        go(h, half, r1_s.at[1, half], r1_r.at[1, half], left1)
    for half in (0, 1):
        ring2(0, half)
    for half in (0, 1):
        to_sibling(0, 0, half)

    landed(piece(1, 0), 0, r1_r.at[0, 0])
    go(piece(1, 0), 0, r1_s.at[2, 0], r1_r.at[2, 0], right1)
    landed(piece(2, 0), 0, r1_r.at[1, 0])
    landed(piece(1, 0), 1, r1_r.at[0, 1])
    landed(piece(2, 0), 1, r1_r.at[1, 1])
    go(piece(2, 0), 1, r1_s.at[2, 1], r1_r.at[2, 1], left1)
    for i1 in (1, 2):
        for half in (0, 1):
            ring2(i1, half)

    def text_landed(cond, slot, half, sem):
        @pl.when(cond)
        def _():
            pltpu.make_async_copy(skv.at[slot, half], skv.at[slot, half], sem).wait()

    for half in (0, 1):
        text_landed(s >= 2, 1, half, tx_r.at[0, half])
        text_landed(core == 1, 0, half, tx_r.at[1, half])
        got = skv.at[1, half]
        guarded((s >= 2) & (core == 0), remote(got, skv.at[2, half], tx_s.at[2, half], tx_r.at[2, half], (sibling, g, e)))
        guarded((s >= 2) & (core == 1), remote(got, skv.at[0, half], tx_s.at[3, half], tx_r.at[3, half], (sibling, g, e)))
        guarded((s >= 2) & (s + 2 < 8), remote(got, skv.at[3, half], tx_s.at[4, half], tx_r.at[4, half], (lax.rem(s + 2, 8), g, e)))

    for half in (0, 1):
        landed(piece(3, 0), half, r1_r.at[2, half])
        ring2(3, half)
    for i1 in (1, 2, 3):
        for half in (0, 1):
            to_sibling(i1, 0, half)

    for i1 in (0, 1, 2, 3):
        landed(piece(i1, 1), 0, r2_r.at[i1, 0, 0])
        go(piece(i1, 1), 0, r2_s.at[i1, 2, 0], r2_r.at[i1, 2, 0], right2)
        to_sibling(i1, 1, 0)
        landed(piece(i1, 2), 0, r2_r.at[i1, 1, 0])
        to_sibling(i1, 2, 0)
        landed(piece(i1, 1), 1, r2_r.at[i1, 0, 1])
        to_sibling(i1, 1, 1)
        landed(piece(i1, 2), 1, r2_r.at[i1, 1, 1])
        go(piece(i1, 2), 1, r2_s.at[i1, 2, 1], r2_r.at[i1, 2, 1], left2)
        to_sibling(i1, 2, 1)
        if i1 == 1:
            for half in (0, 1):
                text_landed((s >= 2) & (core == 1), 2, half, tx_r.at[2, half])
                text_landed((s >= 2) & (core == 0), 0, half, tx_r.at[3, half])
                text_landed(s >= 4, 3, half, tx_r.at[4, half])
                got = skv.at[3, half]
                guarded((s >= 4) & (core == 1), remote(got, skv.at[2, half], tx_s.at[5, half], tx_r.at[5, half], (sibling, g, e)))
    for i1 in (0, 1, 2, 3):
        for half in (0, 1):
            landed(piece(i1, 3), half, r2_r.at[i1, 2, half])
            to_sibling(i1, 3, half)
    for half in (0, 1):
        text_landed((s >= 4) & (core == 0), 2, half, tx_r.at[5, half])

    other = 1 - core
    o1 = e + other * (y - e)
    o2 = y + other * (e - y)
    for i1 in range(4):
        for i2 in range(4):
            q1 = (o1, down(o1), up(o1), lax.rem(o1 + 2, 4))[i1]
            q2 = (o2, down(o2), up(o2), lax.rem(o2 + 2, 4))[i2]
            h = (1 + 7 * other) * q1 + (8 - 7 * other) * q2 + 4 * other
            for half in (0, 1):
                landed(h, half, sib_r.at[i1, i2, half])
    for c in sends:
        c.wait_send()
    for cond, c in text:
        @pl.when(cond)
        def _():
            c.wait_send()


def softmax_step(sc, m_ref, l_ref, a_ref, v, rows):
    n = sc.shape[1] // 128
    m_old = m_ref[rows, :]
    m_new = jnp.maximum(m_old, jnp.max(sc, axis=1, keepdims=True))
    p = jnp.exp2((sc - jnp.concatenate([m_new] * n, axis=1)) * FACTOR)
    alpha = jnp.exp2((m_old - m_new) * FACTOR)
    part = p[:, 0:128]
    for i in range(1, n):
        part = part + p[:, i * 128:(i + 1) * 128]
    l_ref[rows, :] = l_ref[rows, :] * alpha + part
    a_ref[rows, :] = a_ref[rows, :] * alpha + jnp.dot(p.astype(jnp.bfloat16), v, preferred_element_type=jnp.float32)
    m_ref[rows, :] = m_new


def clear(m_ref, l_ref, a_ref, rows):
    m_ref[rows, :] = jnp.full((rows.stop - rows.start, 128), NEG, jnp.float32)
    l_ref[rows, :] = jnp.zeros((rows.stop - rows.start, 128), jnp.float32)
    a_ref[rows, :] = jnp.zeros((rows.stop - rows.start, 128), jnp.float32)


def finish(l_ref, a_ref, rows):
    total = jnp.sum(l_ref[rows, :], axis=1, keepdims=True)
    return (a_ref[rows, :] / jnp.maximum(total, 1.0)).astype(jnp.bfloat16)


def self_kernel(ids_ref, doc_ref, q_ref, k_ref, v_ref, skv_ref, out_ref, qs, os, kbuf, vbuf, bias, m_ref, l_ref, a_ref, q_sem, o_sem, k_sem):
    s = lax.axis_index("seq")
    reads = []
    for i in range(16):
        reads.append(pltpu.make_async_copy(q_ref.at[:, i * 128:(i + 1) * 128], qs.at[i * 256:(i + 1) * 256, :], q_sem.at[i]))
    for d in range(5):
        for half, buf in ((0, kbuf), (1, vbuf)):
            src = (k_ref, v_ref)[half] if d == 0 else skv_ref.at[d - 1, half]
            reads.append(pltpu.make_async_copy(src, buf.at[d * 256:(d + 1) * 256, :], k_sem.at[d, half]))
    for c in reads:
        c.start()

    def row_docs(block):
        return doc_ref[:, pl.ds(pl.multiple_of(block * 256, 256), 256)].astype(jnp.float32)

    own = row_docs(s)
    down = jnp.concatenate(
        [jnp.transpose(jnp.broadcast_to(own[:, i * 128:(i + 1) * 128], (128, 128))) for i in (0, 1)], axis=0
    )
    down = jnp.concatenate([down, down], axis=1)
    rows = lax.broadcasted_iota(jnp.int32, (256, 256), 0)
    cols = lax.broadcasted_iota(jnp.int32, (256, 256), 1)
    bias[:, 0:256] = jnp.where((down == own) & (cols <= rows), 0.0, NEG)
    first = ids_ref[0, s * 256]
    blocks = jnp.int32(1)
    for d in range(1, 5):
        back = jnp.maximum(s - d, 0)
        seen = (s >= d) & (ids_ref[0, back * 256 + 255] == first)
        blocks = blocks + jnp.where(seen, 1, 0)
        bias[:, d * 256:(d + 1) * 256] = jnp.where((down == row_docs(back)) & seen, 0.0, NEG)
    for c in reads:
        c.wait()

    everything = slice(0, 4096)
    clear(m_ref, l_ref, a_ref, everything)

    def chunk(at, size, q):
        cols = slice((q // 2) * 128, (q // 2 + 1) * 128)
        rows = slice(q * 1024, (q + 1) * 1024)
        sc = lax.dot_general(qs[rows, :], kbuf[at, cols], NT, preferred_element_type=jnp.float32)
        sc = sc + jnp.concatenate([bias[:, at]] * 4, axis=0)
        softmax_step(sc, m_ref, l_ref, a_ref, vbuf[at, cols], rows)

    for pair in range(3):
        both = pl.ds(pair * 512, 512)
        one = pl.ds(pair * 512, 256)
        if pair < 2:
            @pl.when(blocks >= 2 * pair + 2)
            def _():
                for q in range(4):
                    chunk(both, 512, q)

        @pl.when(blocks == 2 * pair + 1)
        def _():
            for q in range(4):
                chunk(one, 256, q)
    writes = []
    for i in range(16):
        rows = slice(i * 256, (i + 1) * 256)
        os[rows, :] = finish(l_ref, a_ref, rows)
        c = pltpu.make_async_copy(os.at[rows, :], out_ref.at[:, i * 128:(i + 1) * 128], o_sem.at[i])
        c.start()
        writes.append(c)
    for c in writes:
        c.wait()


def cross_kernel(list_ref, len_ref, mask_ref, q_ref, kv_ref, out_ref, qs, os, kbuf, vbuf, m_ref, l_ref, a_ref, q_sem, o_sem, ksem, vsem):
    s = lax.axis_index("seq")
    e = lax.axis_index("enc")
    per = CHUNK // TILE
    reads = [
        pltpu.make_async_copy(
            q_ref.at[r * 128:(r + 1) * 128, i * 128:(i + 1) * 128],
            qs.at[r * 2048 + i * 128:r * 2048 + (i + 1) * 128, :], q_sem.at[r, i],
        )
        for r in range(2) for i in range(16)
    ]
    for c in reads:
        c.start()

    def tile_copies(r, img, t, pos):
        rows = pl.ds(pl.multiple_of(t * TILE, TILE), TILE)
        to = pl.ds(pl.multiple_of(pos * TILE, TILE), TILE)
        chunk = pos // per
        for half, buf, sem in ((0, kbuf, ksem), (1, vbuf, vsem)):
            pltpu.make_async_copy(
                kv_ref.at[img // 4, half, lax.rem(img, 4), rows, :], buf.at[r, to, :], sem.at[r, chunk]
            ).start()

    def fetch(r):
        def slot(k, pos):
            img = list_ref[e, s, k]
            n = jnp.where(mask_ref[0, r, k] == 1, len_ref[img] // TILE, 0)

            def one(t, p):
                tile_copies(r, img, t, p)
                return p + 1

            return lax.fori_loop(0, n, one, pos)

        n = lax.fori_loop(0, 32, slot, 0)
        chunks = (n + per - 1) // per

        def pad(p, c):
            tile_copies(r, list_ref[e, s, 0], 0, p)
            return c

        lax.fori_loop(n, chunks * per, pad, 0)
        return n

    counts = [fetch(0), fetch(1)]
    for c in reads:
        c.wait()
    writes = []
    for r in range(2):
        n = counts[r]
        clear(m_ref, l_ref, a_ref, slice(0, 2048))

        def chunk(c, size, masked):
            at = pl.ds(pl.multiple_of(c * CHUNK, CHUNK), size)
            whole = pl.ds(pl.multiple_of(c * CHUNK, CHUNK), CHUNK)
            for buf, sem in ((kbuf, ksem), (vbuf, vsem)):
                pltpu.make_async_copy(buf.at[r, whole, :], buf.at[r, whole, :], sem.at[r, c]).wait()
            for j in range(2):
                cols = slice(j * 128, (j + 1) * 128)
                rows = slice(j * 1024, (j + 1) * 1024)
                sc = lax.dot_general(
                    qs[r * 2048 + j * 1024:r * 2048 + (j + 1) * 1024, :], kbuf[r, at, cols], NT,
                    preferred_element_type=jnp.float32,
                )
                if masked:
                    keys = lax.broadcasted_iota(jnp.int32, sc.shape, 1)
                    sc = jnp.where(keys < n * TILE - c * CHUNK, sc, NEG)
                softmax_step(sc, m_ref, l_ref, a_ref, vbuf[r, at, cols], rows)

        full = n // per
        left = n - full * per

        def body(c, carry):
            chunk(c, CHUNK, False)
            return carry

        lax.fori_loop(0, full, body, 0)

        @pl.when(left > per // 2)
        def _():
            chunk(full, CHUNK, True)

        @pl.when((left > 0) & (left <= per // 2))
        def _():
            chunk(full, CHUNK // 2, True)

        for i in range(16):
            rows = slice(i * 128, (i + 1) * 128)
            to = slice(r * 2048 + i * 128, r * 2048 + (i + 1) * 128)
            os[to, :] = finish(l_ref, a_ref, rows)
            c = pltpu.make_async_copy(os.at[to, :], out_ref.at[r * 128:(r + 1) * 128, i * 128:(i + 1) * 128], o_sem.at[r, i])
            c.start()
            writes.append(c)
    for c in writes:
        c.wait()


def local(self_q, self_k, self_v, doc_ids, cross_q, image_keys, image_values, image_list, image_lengths, cross_mask):
    bf16 = jnp.bfloat16
    hbm = pl.BlockSpec(memory_space=pltpu.HBM)
    vm = pl.BlockSpec(memory_space=pltpu.VMEM)
    sm = pl.BlockSpec(memory_space=pltpu.SMEM)
    dma = lambda *shape: pltpu.SemaphoreType.DMA(shape)
    f32 = jnp.float32
    place = lambda x: pltpu.with_memory_space_constraint(x, pltpu.HBM)
    sq, sk, sv, cq = place(self_q[0]), place(self_k[0]), place(self_v[0]), place(cross_q[0])
    kv, skv = pl.pallas_call(
        exchange,
        name="exchange",
        out_shape=(
            pltpu.HBM((32, 2, 4, 128, 256), bf16),
            pltpu.HBM((4, 2, 256, 256), bf16),
        ),
        in_specs=[hbm] * 4,
        out_specs=(hbm, hbm),
        scratch_shapes=[
            dma(3, 2), dma(3, 2), dma(2), dma(3, 2), dma(3, 2), dma(4, 3, 2), dma(4, 3, 2),
            dma(4, 4, 2), dma(4, 4, 2), dma(6, 2), dma(6, 2),
        ],
        compiler_params=pltpu.CompilerParams(collective_id=0, has_side_effects=True, vmem_limit_bytes=1 << 20),
    )(place(image_keys), place(image_values), sk, sv)
    self_out = pl.pallas_call(
        self_kernel,
        name="self_attend",
        out_shape=pltpu.HBM((256, 2048), bf16),
        in_specs=[sm, vm] + [hbm] * 4,
        out_specs=hbm,
        scratch_shapes=[
            pltpu.VMEM((4096, 128), bf16), pltpu.VMEM((4096, 128), bf16),
            pltpu.VMEM((1280, 256), bf16), pltpu.VMEM((1280, 256), bf16), pltpu.VMEM((256, 1280), f32),
            pltpu.VMEM((4096, 128), f32), pltpu.VMEM((4096, 128), f32), pltpu.VMEM((4096, 128), f32),
            dma(16), dma(16), dma(5, 2),
        ],
        compiler_params=pltpu.CompilerParams(vmem_limit_bytes=40 << 20),
    )(doc_ids, doc_ids, sq, sk, sv, place(skv))
    cross_out = pl.pallas_call(
        cross_kernel,
        name="cross_attend",
        out_shape=pltpu.HBM((256, 2048), bf16),
        in_specs=[sm, sm, sm, hbm, hbm],
        out_specs=hbm,
        scratch_shapes=[
            pltpu.VMEM((4096, 128), bf16), pltpu.VMEM((4096, 128), bf16),
            pltpu.VMEM((2, 4096, 256), bf16), pltpu.VMEM((2, 4096, 256), bf16),
            pltpu.VMEM((2048, 128), f32), pltpu.VMEM((2048, 128), f32), pltpu.VMEM((2048, 128), f32),
            dma(2, 16), dma(2, 16), dma(2, 4096 // CHUNK), dma(2, 4096 // CHUNK),
        ],
        compiler_params=pltpu.CompilerParams(vmem_limit_bytes=40 << 20),
    )(image_list, image_lengths, cross_mask, cq, kv)
    return self_out[None], cross_out[None]


def solution(mesh):
    in_specs = (
        P("enc", "seq", "mp"),
        P("enc", "seq", "mp"),
        P("enc", "seq", "mp"),
        P("enc", None),
        P("enc", "seq", "mp"),
        P(("seq", "enc"), "mp", None),
        P(("seq", "enc"), "mp", None),
        P(),
        P(),
        P("enc", "seq", None),
    )
    out_specs = (P("enc", "seq", "mp"), P("enc", "seq", "mp"))
    return jax.shard_map(local, mesh=mesh, in_specs=in_specs, out_specs=out_specs, check_vma=False)
```

```python
import functools
import jax
import jax.numpy as jnp
from jax import lax
from jax.experimental import pallas as pl
from jax.experimental.pallas import tpu as pltpu
from jax.sharding import PartitionSpec as P

HD = 128
NEG = -1e30
START = -5e29
LOG2E = 1.4426950408889634
FACTOR = HD ** (-0.5) * LOG2E
MESH = pl.DeviceIdType.MESH
TILE = 32
NT = (((1,), (1,)), ((), ()))


def softmax_step(sc, m_ref, l_ref, a_ref, v, rows):
    n = sc.shape[1] // 128
    m_old = m_ref[rows, :]
    m_new = jnp.maximum(m_old, jnp.max(sc, axis=1, keepdims=True))
    p = jnp.exp2((sc - jnp.concatenate([m_new] * n, axis=1)) * FACTOR)
    alpha = jnp.exp2((m_old - m_new) * FACTOR)
    part = p[:, 0:128]
    for i in range(1, n):
        part = part + p[:, i * 128:(i + 1) * 128]
    l_ref[rows, :] = l_ref[rows, :] * alpha + part
    a_ref[rows, :] = a_ref[rows, :] * alpha + jnp.dot(p.astype(jnp.bfloat16), v, preferred_element_type=jnp.float32)
    m_ref[rows, :] = m_new


def whole(
    ik, iv, sk, sv, ids, sq, cq, lists, lengths, flags, self_out, cross_out,
    kv0, kv1, kv2, kv3, qs, qc, os, kbuf, vbuf, kst, vst, docs, bias, row_bias, m_ref, l_ref, a_ref,
    list_s, len_s, flag_s,
    mp_s, mp_r, own_s, r1_s, r1_r, r2_s, r2_r, sib_s, sib_r, tx_s, tx_r, load_sem, out_sem,
):
    kv = (kv0, kv1, kv2, kv3)
    s = lax.axis_index("seq")
    g = lax.axis_index("mp")
    e = lax.axis_index("enc")
    core = lax.rem(s, 2)
    y = s // 2
    sibling = (s + 1 - 2 * core, g, e)
    me = s * 4 + e

    def place(c):
        return e + c * (y - e), y + c * (e - y)

    p1, p2 = place(core)
    up = lambda p: lax.rem(p + 1, 4)
    down = lambda p: lax.rem(p + 3, 4)
    steps = (lambda p: p, down, up, lambda p: lax.rem(p + 2, 4))

    def at(q1, q2):
        return (2 * (q2 + core * (q1 - q2)) + core, g, q1 + core * (q2 - q1))

    def piece(i1, i2, c=core):
        q1, q2 = place(c)
        return ((1 + 7 * c) * steps[i1](q1) + (8 - 7 * c) * steps[i2](q2) + 4 * c) * 4

    right1, left1 = at(up(p1), p2), at(down(p1), p2)
    right2, left2 = at(p1, up(p2)), at(p1, down(p2))

    loads = [
        pltpu.make_async_copy(lists, list_s, load_sem.at[0]),
        pltpu.make_async_copy(lengths, len_s, load_sem.at[1]),
        pltpu.make_async_copy(flags, flag_s, load_sem.at[2]),
        pltpu.make_async_copy(ids, docs, load_sem.at[3]),
        pltpu.make_async_copy(sk, kbuf.at[0:256, :], load_sem.at[4]),
        pltpu.make_async_copy(sv, vbuf.at[0:256, :], load_sem.at[5]),
    ]
    for i in range(16):
        loads.append(pltpu.make_async_copy(sq.at[:, i * 128:(i + 1) * 128], qs.at[i * 256:(i + 1) * 256, :], load_sem.at[6 + i]))
    late = []
    for r in range(2):
        for i in range(16):
            late.append(pltpu.make_async_copy(
                cq.at[r * 128:(r + 1) * 128, i * 128:(i + 1) * 128],
                qc.at[r * 2048 + i * 128:r * 2048 + (i + 1) * 128, :], load_sem.at[22 + r * 16 + i],
            ))

    barrier = pltpu.get_barrier_semaphore()
    greet = [right1, left1, right2, left2, sibling] + [(s, lax.rem(g + d, 4), e) for d in (1, 2, 3)]
    for who in greet:
        pl.semaphore_signal(barrier, inc=1, device_id=who, device_id_type=MESH)
    for c in loads:
        c.start()
    pl.semaphore_wait(barrier, len(greet))

    def remote(src, dst, ss, rs, who):
        return pltpu.make_async_remote_copy(
            src_ref=src, dst_ref=dst, send_sem=ss, recv_sem=rs, device_id=who, device_id_type=MESH
        )

    sends = []

    def go(cond, r):
        sends.append((cond, r))
        if cond is None:
            r.start()
        else:
            @pl.when(cond)
            def _():
                r.start()

    def landed(t, first, count, rs):
        ref = kv[t].at[pl.ds(first, count)]
        pltpu.make_async_copy(ref, ref, rs).wait()

    for t in range(4):
        for half, src in ((0, ik), (1, iv)):
            for d in (1, 2, 3):
                to = (t + d) % 4
                go(g == t, remote(
                    src.at[:, :, to * 256:(to + 1) * 256],
                    kv[t].at[pl.ds(me * 4, 4), half], mp_s.at[t, d - 1, half], mp_r.at[t, half], (s, to, e),
                ))

            @pl.when(g == t)
            def _():
                pltpu.make_async_copy(
                    src.at[:, :, t * 256:(t + 1) * 256], kv[t].at[pl.ds(me * 4, 4), half], own_s.at[half]
                ).start()

    def text_at(buf, d):
        return buf.at[256 * d:256 * (d + 1), :]

    def text_landed(cond, d, half, sem):
        @pl.when(cond)
        def _():
            ref = text_at((kbuf, vbuf)[half], d)
            pltpu.make_async_copy(ref, ref, sem).wait()

    ahead = (lax.rem(s + 2, 8), g, e)
    for half, src in ((0, sk), (1, sv)):
        buf = (kbuf, vbuf)[half]
        go(s + 2 < 8, remote(src, text_at(buf, 2), tx_s.at[0, half], tx_r.at[0, half], ahead))
        go(core == 0, remote(src, text_at(buf, 1), tx_s.at[1, half], tx_r.at[1, half], sibling))
    for d in range(1, 5):
        @pl.when(s < d)
        def _():
            for buf in (kbuf, vbuf):
                buf[256 * d:256 * (d + 1), :] = jnp.zeros((256, 256), jnp.bfloat16)

    def text_onward():
        for half in (0, 1):
            buf = (kbuf, vbuf)[half]
            text_landed(s >= 2, 2, half, tx_r.at[0, half])
            got = text_at(buf, 2)
            go((s >= 2) & (s + 2 < 8), remote(got, text_at(buf, 4), tx_s.at[4, half], tx_r.at[4, half], ahead))
            go((s >= 2) & (core == 0), remote(got, text_at(buf, 3), tx_s.at[2, half], tx_r.at[2, half], sibling))
            go((s >= 2) & (core == 1), remote(got, text_at(buf, 1), tx_s.at[3, half], tx_r.at[3, half], sibling))

    def text_near():
        for half in (0, 1):
            text_landed(core == 1, 1, half, tx_r.at[1, half])
            text_landed((s >= 2) & (core == 0), 1, half, tx_r.at[3, half])

    def text_far():
        for half in (0, 1):
            buf = (kbuf, vbuf)[half]
            text_landed(s >= 4, 4, half, tx_r.at[4, half])
            go((s >= 4) & (core == 1), remote(text_at(buf, 4), text_at(buf, 3), tx_s.at[5, half], tx_r.at[5, half], sibling))
        for half in (0, 1):
            text_landed((s >= 2) & (core == 1), 3, half, tx_r.at[2, half])
            text_landed((s >= 4) & (core == 0), 3, half, tx_r.at[5, half])

    def send(t, first, count, ss, rs, who, cond=None):
        ref = kv[t].at[pl.ds(first, count)]
        go(cond, remote(ref, ref, ss, rs, who))

    def to_sibling(i1, i2, t):
        send(t, piece(i1, i2), 4, sib_s.at[i1, i2, t], sib_r.at[i1, i2, t], sibling)

    def ring2(i1, t):
        h = piece(i1, 0)
        send(t, h, 4, r2_s.at[i1, 0, t], r2_r.at[i1, 0, t], right2)
        send(t, h, 4, r2_s.at[i1, 1, t], r2_r.at[i1, 1, t], left2)

    def ready(t):
        for half in (0, 1):
            ref = kv[t].at[pl.ds(me * 4, 4), half]

            @pl.when(g == t)
            def _():
                pltpu.make_async_copy(ref, ref, own_s.at[half]).wait()

            @pl.when(g != t)
            def _():
                pltpu.make_async_copy(ref, ref, mp_r.at[t, half]).wait()
        h = piece(0, 0)
        send(t, h, 4, r1_s.at[0, t], r1_r.at[0, t], right1)
        send(t, h, 4, r1_s.at[1, t], r1_r.at[1, t], left1)
        ring2(0, t)
        to_sibling(0, 0, t)

    def near1(t):
        for i1, to in ((1, right1), (2, left1)):
            h = piece(i1, 0)
            landed(t, h, 4, r1_r.at[i1 - 1, t])
            send(t, h + 2 * (i1 - 1), 2, r1_s.at[1 + i1, t], r1_r.at[1 + i1, t], to)
            ring2(i1, t)
            to_sibling(i1, 0, t)

    def far1(t):
        h = piece(3, 0)
        landed(t, h, 2, r1_r.at[2, t])
        landed(t, h + 2, 2, r1_r.at[3, t])
        ring2(3, t)
        to_sibling(3, 0, t)

    def near2(i1, t):
        both = None if t > 1 else core == 1
        h = piece(i1, 1)
        landed(t, h, 4, r2_r.at[i1, 0, t])
        send(t, h, 2, r2_s.at[i1, 2, t], r2_r.at[i1, 2, t], right2, both)
        to_sibling(i1, 1, t)
        h = piece(i1, 2)
        landed(t, h, 4, r2_r.at[i1, 1, t])
        if t <= 1:
            send(t, h, 2, r2_s.at[i1, 2, t], r2_r.at[i1, 2, t], left2, core == 0)
        send(t, h + 2, 2, r2_s.at[i1, 3, t], r2_r.at[i1, 3, t], left2)
        to_sibling(i1, 2, t)

    def far2(t):
        for i1 in range(4):
            h = piece(i1, 3)
            landed(t, h, 2, r2_r.at[i1, 2, t])
            landed(t, h + 2, 2, r2_r.at[i1, 3, t])
            to_sibling(i1, 3, t)

    def from_sibling(t):
        for i1 in range(4):
            for i2 in range(4):
                landed(t, piece(i1, i2, 1 - core), 4, sib_r.at[i1, i2, t])

    def self_setup():
        for c in loads:
            c.wait()
        for c in late:
            c.start()

        def row_docs(block):
            return docs[:, pl.ds(pl.multiple_of(block * 256, 256), 256)].astype(jnp.float32)

        own = row_docs(s)
        column = jnp.concatenate(
            [jnp.transpose(jnp.broadcast_to(own[:, i * 128:(i + 1) * 128], (128, 128))) for i in (0, 1)], axis=0
        )
        column = jnp.concatenate([column, column], axis=1)
        rows = lax.broadcasted_iota(jnp.int32, (256, 256), 0)
        cols = lax.broadcasted_iota(jnp.int32, (256, 256), 1)
        bias[:, 0:256] = jnp.where((column == own) & (cols <= rows), 0.0, NEG)
        for d in range(1, 5):
            seen = (column == row_docs(jnp.maximum(s - d, 0))) & (rows - rows + s >= d)
            bias[:, d * 256:(d + 1) * 256] = jnp.where(seen, 0.0, NEG)

    def clear():
        m_ref[...] = jnp.full_like(m_ref, START)
        l_ref[...] = jnp.zeros_like(l_ref)
        a_ref[...] = jnp.zeros_like(a_ref)

    def self_units(lo, hi, key, size):
        def unit(q, carry):
            cols = pl.ds(pl.multiple_of(q // 2 * 128, 128), 128)
            rows = pl.ds(pl.multiple_of(q * 1024, 1024), 1024)
            sc = lax.dot_general(qs[rows, :], kbuf[key:key + size, cols], NT, preferred_element_type=jnp.float32)
            sc = sc + jnp.concatenate([bias[:, key:key + size]] * 4, axis=0)
            softmax_step(sc, m_ref, l_ref, a_ref, vbuf[key:key + size, cols], rows)
            return carry

        lax.fori_loop(lo, hi, unit, 0)

    writes = []

    def emit(out, tokens, which):
        for i in range(4096 // tokens):
            rows = slice(i * tokens, (i + 1) * tokens)
            total = jnp.sum(l_ref[rows, :], axis=1, keepdims=True)
            os[rows, :] = (a_ref[rows, :] / jnp.maximum(total, 1.0)).astype(jnp.bfloat16)
            r, h = (0, i) if tokens == 256 else (i // 16, i % 16)
            c = pltpu.make_async_copy(
                os.at[rows, :], out.at[r * tokens:(r + 1) * tokens, h * 128:(h + 1) * 128], out_sem.at[which, i]
            )
            c.start()
            writes.append(c)

    def drain():
        for c in writes:
            c.wait()
        writes.clear()

    def stage(t):
        slot_of = lax.broadcasted_iota(jnp.int32, (8, 1024), 1) // TILE

        def one(k, lines):
            img = list_s[e, s, k]
            to = pl.ds(pl.multiple_of(k * TILE, TILE), TILE)
            kst[to, :] = kv[t][img, 0]
            vst[to, :] = kv[t][img, 1]
            live = len_s[img] > t * TILE
            return tuple(
                jnp.where((slot_of == k) & live & (flag_s[0, r, k] == 1), 0.0, lines[r]) for r in (0, 1)
            )

        empty = jnp.full((8, 1024), NEG, jnp.float32)
        for r, line in enumerate(lax.fori_loop(0, 32, one, (empty, empty))):
            row_bias[8 * r:8 * (r + 1), :] = line

    def cross_units(lo, hi):
        def unit(u, carry):
            half = lax.rem(u, 2)
            rj = u // 2
            keys = pl.ds(pl.multiple_of(half * 512, 512), 512)
            cols = pl.ds(pl.multiple_of(lax.rem(rj, 2) * 128, 128), 128)
            rows = pl.ds(pl.multiple_of(rj * 1024, 1024), 1024)
            sc = lax.dot_general(qc[rows, :], kst[keys, cols], NT, preferred_element_type=jnp.float32)
            line = row_bias[pl.ds(pl.multiple_of(rj // 2 * 8, 8), 8), keys]
            sc = sc + jnp.concatenate([line] * 128, axis=0)
            softmax_step(sc, m_ref, l_ref, a_ref, vst[keys, cols], rows)
            return carry

        lax.fori_loop(lo, hi, unit, 0)

    self_setup()
    clear()
    ready(0)
    ready(1)
    text_onward()
    near1(0)
    text_near()
    self_units(0, 2, 0, 512)
    near2(0, 0)
    near1(1)
    self_units(2, 4, 0, 512)
    far1(0)
    ready(2)
    text_far()
    self_units(0, 2, 512, 512)
    near2(1, 0)
    near2(2, 0)
    near2(0, 1)
    self_units(2, 4, 512, 512)
    far1(1)
    near2(3, 0)
    near1(2)
    self_units(0, 4, 1024, 256)
    emit(self_out, 256, 0)
    for c in late:
        c.wait()
    near2(1, 1)
    near2(2, 1)
    far2(0)
    ready(3)
    clear()
    from_sibling(0)
    stage(0)
    cross_units(0, 2)
    near2(0, 2)
    far1(2)
    near1(3)
    cross_units(2, 4)
    near2(3, 1)
    near2(1, 2)
    cross_units(4, 6)
    near2(2, 2)
    far2(1)
    near2(0, 3)
    cross_units(6, 8)
    far1(3)
    near2(3, 2)
    from_sibling(1)
    stage(1)
    cross_units(0, 2)
    near2(1, 3)
    near2(2, 3)
    cross_units(2, 4)
    far2(2)
    near2(3, 3)
    cross_units(4, 8)
    from_sibling(2)
    stage(2)
    cross_units(0, 2)
    far2(3)
    cross_units(2, 8)
    from_sibling(3)
    stage(3)
    drain()
    cross_units(0, 8)
    emit(cross_out, 128, 1)
    for cond, r in sends:
        if cond is None:
            r.wait_send()
        else:
            @pl.when(cond)
            def _():
                r.wait_send()
    drain()


def local(self_q, self_k, self_v, doc_ids, cross_q, image_keys, image_values, image_list, image_lengths, cross_mask):
    bf16, f32, i32 = jnp.bfloat16, jnp.float32, jnp.int32
    hbm = pl.BlockSpec(memory_space=pltpu.HBM)
    dma = lambda *shape: pltpu.SemaphoreType.DMA(shape)
    place = lambda x: pltpu.with_memory_space_constraint(x, pltpu.HBM)
    args = (
        image_keys, image_values, self_k[0], self_v[0], doc_ids, self_q[0], cross_q[0], image_list, image_lengths, cross_mask,
    )
    self_out, cross_out = pl.pallas_call(
        whole,
        name="whole",
        out_shape=(pltpu.HBM((256, 2048), bf16), pltpu.HBM((256, 2048), bf16)),
        in_specs=[hbm] * 10,
        out_specs=(hbm, hbm),
        scratch_shapes=[pltpu.VMEM((128, 2, TILE, 256), bf16)] * 4 + [
            pltpu.VMEM((4096, 128), bf16), pltpu.VMEM((4096, 128), bf16), pltpu.VMEM((4096, 128), bf16),
            pltpu.VMEM((1280, 256), bf16), pltpu.VMEM((1280, 256), bf16),
            pltpu.VMEM((1024, 256), bf16), pltpu.VMEM((1024, 256), bf16),
            pltpu.VMEM((1, 2048), i32), pltpu.VMEM((256, 1280), f32), pltpu.VMEM((16, 1024), f32),
            pltpu.VMEM((4096, 128), f32), pltpu.VMEM((4096, 128), f32), pltpu.VMEM((4096, 128), f32),
            pltpu.SMEM((4, 8, 32), i32), pltpu.SMEM((128,), i32), pltpu.SMEM((1, 2, 32), i32),
            dma(4, 3, 2), dma(4, 2), dma(2), dma(4, 4), dma(4, 4), dma(4, 4, 4), dma(4, 4, 4),
            dma(4, 4, 4), dma(4, 4, 4), dma(6, 2), dma(6, 2), dma(54), dma(2, 32),
        ],
        compiler_params=pltpu.CompilerParams(collective_id=0, has_side_effects=True, vmem_limit_bytes=56 << 20),
    )(*(place(x) for x in args))
    return self_out[None], cross_out[None]


def solution(mesh):
    in_specs = (
        P("enc", "seq", "mp"),
        P("enc", "seq", "mp"),
        P("enc", "seq", "mp"),
        P("enc", None),
        P("enc", "seq", "mp"),
        P(("seq", "enc"), "mp", None),
        P(("seq", "enc"), "mp", None),
        P(),
        P(),
        P("enc", "seq", None),
    )
    out_specs = (P("enc", "seq", "mp"), P("enc", "seq", "mp"))
    return jax.shard_map(local, mesh=mesh, in_specs=in_specs, out_specs=out_specs, check_vma=False)
```

```python
import functools
import jax
import jax.numpy as jnp
from jax import lax
from jax.experimental import pallas as pl
from jax.experimental.pallas import tpu as pltpu
from jax.sharding import PartitionSpec as P

HD = 128
NEG = -1e30
START = -5e29
LOG2E = 1.4426950408889634
FACTOR = HD ** (-0.5) * LOG2E
MESH = pl.DeviceIdType.MESH
TILE = 32
CHUNK = 512
NT = (((1,), (1,)), ((), ()))


def softmax_step(sc, m_ref, l_ref, a_ref, v, rows):
    n = sc.shape[1] // 128
    m_old = m_ref[rows, :]
    m_new = jnp.maximum(m_old, jnp.max(sc, axis=1, keepdims=True))
    p = jnp.exp2((sc - jnp.concatenate([m_new] * n, axis=1)) * FACTOR)
    alpha = jnp.exp2((m_old - m_new) * FACTOR)
    part = p[:, 0:128]
    for i in range(1, n):
        part = part + p[:, i * 128:(i + 1) * 128]
    l_ref[rows, :] = l_ref[rows, :] * alpha + part
    a_ref[rows, :] = a_ref[rows, :] * alpha + jnp.dot(p.astype(jnp.bfloat16), v, preferred_element_type=jnp.float32)
    m_ref[rows, :] = m_new


def clear(m_ref, l_ref, a_ref):
    m_ref[...] = jnp.full_like(m_ref, START)
    l_ref[...] = jnp.zeros_like(l_ref)
    a_ref[...] = jnp.zeros_like(a_ref)


def exchange(
    ik, iv, sk, sv, ids, sq, kv, self_out, qs, os, kbuf, vbuf, docs, bias, m_ref, l_ref, a_ref,
    mp_s, mp_r, own_s, r1_s, r1_r, r2_s, r2_r, sib_s, sib_r, tx_s, tx_r, load_sem, out_sem,
):
    s = lax.axis_index("seq")
    g = lax.axis_index("mp")
    e = lax.axis_index("enc")
    core = lax.rem(s, 2)
    y = s // 2
    sibling = (s + 1 - 2 * core, g, e)
    me = s * 4 + e

    def place(c):
        return e + c * (y - e), y + c * (e - y)

    p1, p2 = place(core)
    up = lambda p: lax.rem(p + 1, 4)
    down = lambda p: lax.rem(p + 3, 4)
    steps = (lambda p: p, down, up, lambda p: lax.rem(p + 2, 4))

    def at(q1, q2):
        return (2 * (q2 + core * (q1 - q2)) + core, g, q1 + core * (q2 - q1))

    def piece(i1, i2, c=core):
        q1, q2 = place(c)
        return (1 + 7 * c) * steps[i1](q1) + (8 - 7 * c) * steps[i2](q2) + 4 * c

    right1, left1 = at(up(p1), p2), at(down(p1), p2)
    right2, left2 = at(p1, up(p2)), at(p1, down(p2))

    loads = [
        pltpu.make_async_copy(ids, docs, load_sem.at[0]),
        pltpu.make_async_copy(sk, kbuf.at[0:256, :], load_sem.at[1]),
        pltpu.make_async_copy(sv, vbuf.at[0:256, :], load_sem.at[2]),
    ]
    for i in range(16):
        loads.append(pltpu.make_async_copy(sq.at[:, i * 128:(i + 1) * 128], qs.at[i * 256:(i + 1) * 256, :], load_sem.at[3 + i]))

    barrier = pltpu.get_barrier_semaphore()
    greet = [right1, left1, right2, left2, sibling] + [(s, lax.rem(g + d, 4), e) for d in (1, 2, 3)]
    for who in greet:
        pl.semaphore_signal(barrier, inc=1, device_id=who, device_id_type=MESH)
    for c in loads:
        c.start()
    pl.semaphore_wait(barrier, len(greet))

    def remote(src, dst, ss, rs, who):
        return pltpu.make_async_remote_copy(
            src_ref=src, dst_ref=dst, send_sem=ss, recv_sem=rs, device_id=who, device_id_type=MESH
        )

    sends = []

    def go(h, c, ss, rs, who):
        r = remote(kv.at[h, c], kv.at[h, c], ss, rs, who)
        r.start()
        sends.append(r)

    def landed(h, c, rs):
        pltpu.make_async_copy(kv.at[h, c], kv.at[h, c], rs).wait()

    mine = pl.ds(pl.multiple_of(g * TILE, TILE), TILE)
    first = []
    for c in range(4):
        group = []
        for d in (1, 2, 3, 0):
            to = lax.rem(g + d, 4)
            cols = pl.ds(pl.multiple_of(to * 256, 256), 256)
            for half, src in ((0, ik), (1, iv)):
                a, b = src.at[c, :, cols], kv.at[me, c, half, mine, :]
                if d:
                    r = remote(a, b, mp_s.at[d - 1, c, half], mp_r.at[d - 1, c, half], (s, to, e))
                else:
                    r = pltpu.make_async_copy(a, b, own_s.at[c, half])
                r.start()
                group.append(r)
        first.append(group)

    text = []

    def guarded(cond, r):
        text.append((cond, r))

        @pl.when(cond)
        def _():
            r.start()

    def text_at(buf, d):
        return buf.at[256 * d:256 * (d + 1), :]

    def text_landed(cond, d, half, sem):
        @pl.when(cond)
        def _():
            ref = text_at((kbuf, vbuf)[half], d)
            pltpu.make_async_copy(ref, ref, sem).wait()

    ahead = (lax.rem(s + 2, 8), g, e)
    for half, src in ((0, sk), (1, sv)):
        buf = (kbuf, vbuf)[half]
        guarded(s + 2 < 8, remote(src, text_at(buf, 2), tx_s.at[0, half], tx_r.at[0, half], ahead))
        guarded(core == 0, remote(src, text_at(buf, 1), tx_s.at[1, half], tx_r.at[1, half], sibling))
    for d in range(1, 5):
        @pl.when(s < d)
        def _():
            for buf in (kbuf, vbuf):
                buf[256 * d:256 * (d + 1), :] = jnp.zeros((256, 256), jnp.bfloat16)

    def text_onward():
        for half in (0, 1):
            buf = (kbuf, vbuf)[half]
            text_landed(s >= 2, 2, half, tx_r.at[0, half])
            got = text_at(buf, 2)
            guarded((s >= 2) & (s + 2 < 8), remote(got, text_at(buf, 4), tx_s.at[4, half], tx_r.at[4, half], ahead))
            guarded((s >= 2) & (core == 0), remote(got, text_at(buf, 3), tx_s.at[2, half], tx_r.at[2, half], sibling))
            guarded((s >= 2) & (core == 1), remote(got, text_at(buf, 1), tx_s.at[3, half], tx_r.at[3, half], sibling))

    def text_near():
        for half in (0, 1):
            text_landed(core == 1, 1, half, tx_r.at[1, half])
            text_landed((s >= 2) & (core == 0), 1, half, tx_r.at[3, half])

    def text_far():
        for half in (0, 1):
            buf = (kbuf, vbuf)[half]
            text_landed(s >= 4, 4, half, tx_r.at[4, half])
            guarded((s >= 4) & (core == 1), remote(text_at(buf, 4), text_at(buf, 3), tx_s.at[5, half], tx_r.at[5, half], sibling))
        for half in (0, 1):
            text_landed((s >= 2) & (core == 1), 3, half, tx_r.at[2, half])
            text_landed((s >= 4) & (core == 0), 3, half, tx_r.at[5, half])

    def to_sibling(i1, i2, c):
        go(piece(i1, i2), c, sib_s.at[i1, i2, c], sib_r.at[i1, i2, c], sibling)

    def ring1(c):
        h = piece(0, 0)
        go(h, c, r1_s.at[0, c], r1_r.at[0, c], right1)
        go(h, c, r1_s.at[1, c], r1_r.at[1, c], left1)

    def ring2(i1, c):
        h = piece(i1, 0)
        go(h, c, r2_s.at[i1, 0, c], r2_r.at[i1, 0, c], right2)
        go(h, c, r2_s.at[i1, 1, c], r2_r.at[i1, 1, c], left2)

    def onward1(c):
        for i1, far, to in ((1, c < 2, right1), (2, c >= 2, left1)):
            landed(piece(i1, 0), c, r1_r.at[i1 - 1, c])
            if far:
                go(piece(i1, 0), c, r1_s.at[2, c], r1_r.at[2, c], to)
            ring2(i1, c)
            to_sibling(i1, 0, c)

    def onward2(i1, c):
        for i2, far, to in ((1, c < 1, right2), (2, c >= 1, left2)):
            landed(piece(i1, i2), c, r2_r.at[i1, i2 - 1, c])
            if far:
                go(piece(i1, i2), c, r2_s.at[i1, 2, c], r2_r.at[i1, 2, c], to)
            to_sibling(i1, i2, c)

    def self_setup():
        for c in loads:
            c.wait()

        def row_docs(block):
            return docs[:, pl.ds(pl.multiple_of(block * 256, 256), 256)].astype(jnp.float32)

        own = row_docs(s)
        column = jnp.concatenate(
            [jnp.transpose(jnp.broadcast_to(own[:, i * 128:(i + 1) * 128], (128, 128))) for i in (0, 1)], axis=0
        )
        column = jnp.concatenate([column, column], axis=1)
        rows = lax.broadcasted_iota(jnp.int32, (256, 256), 0)
        cols = lax.broadcasted_iota(jnp.int32, (256, 256), 1)
        bias[:, 0:256] = jnp.where((column == own) & (cols <= rows), 0.0, NEG)
        for d in range(1, 5):
            seen = (column == row_docs(jnp.maximum(s - d, 0))) & (rows - rows + s >= d)
            bias[:, d * 256:(d + 1) * 256] = jnp.where(seen, 0.0, NEG)

    def self_units(lo, hi, key, size):
        def unit(q, carry):
            cols = pl.ds(pl.multiple_of(q // 2 * 128, 128), 128)
            rows = pl.ds(pl.multiple_of(q * 1024, 1024), 1024)
            sc = lax.dot_general(qs[rows, :], kbuf[key:key + size, cols], NT, preferred_element_type=jnp.float32)
            sc = sc + jnp.concatenate([bias[:, key:key + size]] * 4, axis=0)
            softmax_step(sc, m_ref, l_ref, a_ref, vbuf[key:key + size, cols], rows)
            return carry

        lax.fori_loop(lo, hi, unit, 0)

    writes = []

    def emit():
        for i in range(16):
            rows = slice(i * 256, (i + 1) * 256)
            total = jnp.sum(l_ref[rows, :], axis=1, keepdims=True)
            os[rows, :] = (a_ref[rows, :] / jnp.maximum(total, 1.0)).astype(jnp.bfloat16)
            c = pltpu.make_async_copy(os.at[rows, :], self_out.at[:, i * 128:(i + 1) * 128], out_sem.at[i])
            c.start()
            writes.append(c)

    for c in range(4):
        for r in first[c]:
            r.wait()
        ring1(c)
        ring2(0, c)
        to_sibling(0, 0, c)
    self_setup()
    clear(m_ref, l_ref, a_ref)
    text_onward()
    onward1(0)
    onward2(0, 0)
    text_near()
    self_units(0, 1, 0, 512)
    onward1(1)
    onward2(0, 1)
    self_units(1, 2, 0, 512)
    onward1(2)
    onward2(0, 2)
    self_units(2, 3, 0, 512)
    onward1(3)
    onward2(0, 3)
    self_units(3, 4, 0, 512)
    text_far()
    for c in range(4):
        landed(piece(3, 0), c, r1_r.at[2, c])
        ring2(3, c)
        to_sibling(3, 0, c)
        for i1 in (1, 2):
            onward2(i1, c)
        self_units(c, c + 1, 512, 512)
    for c in range(4):
        onward2(3, c)
        self_units(c, c + 1, 1024, 256)
    emit()
    for i1 in range(4):
        for c in range(4):
            landed(piece(i1, 3), c, r2_r.at[i1, 2, c])
            to_sibling(i1, 3, c)

    for i1 in range(4):
        for i2 in range(4):
            for c in range(4):
                landed(piece(i1, i2, 1 - core), c, sib_r.at[i1, i2, c])
    for r in sends:
        r.wait_send()
    for cond, r in text:
        @pl.when(cond)
        def _():
            r.wait_send()
    for c in writes:
        c.wait()


def cross_kernel(lists, lengths, flags, q_ref, kv_ref, done, out_ref, self_ref, list_ref, len_ref, mask_ref, qs, os, buf, m_ref, l_ref, a_ref, t_sem, q_sem, o_sem, kv_sem, d_sem):
    s = lax.axis_index("seq")
    e = lax.axis_index("enc")
    per = CHUNK // TILE
    tables = [
        pltpu.make_async_copy(lists, list_ref, t_sem.at[0]),
        pltpu.make_async_copy(lengths, len_ref, t_sem.at[1]),
        pltpu.make_async_copy(flags, mask_ref, t_sem.at[2]),
    ]
    reads = [
        pltpu.make_async_copy(
            q_ref.at[r * 128:(r + 1) * 128, i * 128:(i + 1) * 128],
            qs.at[r * 2048 + i * 128:r * 2048 + (i + 1) * 128, :], q_sem.at[r, i],
        )
        for r in range(2) for i in range(16)
    ]
    carried = [
        pltpu.make_async_copy(done.at[i * 64:(i + 1) * 64, :], self_ref.at[i * 64:(i + 1) * 64, :], d_sem.at[i])
        for i in range(4)
    ]
    for c in tables + reads + carried:
        c.start()
    for c in tables:
        c.wait()

    def fetch(r):
        def slot(k, pos):
            img = list_ref[e, s, k]
            n = jnp.where(mask_ref[0, r, k] == 1, len_ref[img] // TILE, 0)
            for size in range(1, 5):
                @pl.when(n == size)
                def _():
                    pltpu.make_async_copy(
                        kv_ref.at[img // 4, lax.rem(img, 4), :, 0:size * TILE, :],
                        buf.at[r, :, pl.ds(pl.multiple_of(pos * TILE, TILE), size * TILE), :], kv_sem.at[r],
                    ).start()
            return pos + n

        return lax.fori_loop(0, 32, slot, 0)

    counts = [fetch(0), fetch(1)]
    writes = []
    for r in range(2):
        n = counts[r]
        clear(m_ref, l_ref, a_ref)
        if r == 0:
            for c in reads:
                c.wait()

        def arrived(p, carry):
            ref = buf.at[r, :, 0:TILE, :]
            pltpu.make_async_copy(ref, ref, kv_sem.at[r]).wait()
            return carry

        lax.fori_loop(0, n, arrived, 0)

        def blank(p, carry):
            buf[r, 1, pl.ds(pl.multiple_of(p * TILE, TILE), TILE), :] = jnp.zeros((TILE, 256), jnp.bfloat16)
            return carry

        lax.fori_loop(n, (n + 7) // 8 * 8, blank, 0)

        def chunk(c, size, masked):
            at = pl.ds(pl.multiple_of(c * CHUNK, CHUNK), size)
            for j in range(2):
                cols = slice(j * 128, (j + 1) * 128)
                rows = slice(j * 1024, (j + 1) * 1024)
                sc = lax.dot_general(
                    qs[r * 2048 + j * 1024:r * 2048 + (j + 1) * 1024, :], buf[r, 0, at, cols], NT,
                    preferred_element_type=jnp.float32,
                )
                if masked:
                    keys = lax.broadcasted_iota(jnp.int32, sc.shape, 1)
                    sc = jnp.where(keys < n * TILE - c * CHUNK, sc, NEG)
                softmax_step(sc, m_ref, l_ref, a_ref, buf[r, 1, at, cols], rows)

        full = n // per
        left = n - full * per

        def body(c, carry):
            chunk(c, CHUNK, False)
            return carry

        lax.fori_loop(0, full, body, 0)

        @pl.when(left > per // 2)
        def _():
            chunk(full, CHUNK, True)

        @pl.when((left > 0) & (left <= per // 2))
        def _():
            chunk(full, CHUNK // 2, True)

        for i in range(16):
            rows = slice(i * 128, (i + 1) * 128)
            to = slice(r * 2048 + i * 128, r * 2048 + (i + 1) * 128)
            total = jnp.sum(l_ref[rows, :], axis=1, keepdims=True)
            os[to, :] = (a_ref[rows, :] / jnp.maximum(total, 1.0)).astype(jnp.bfloat16)
            c = pltpu.make_async_copy(os.at[to, :], out_ref.at[r * 128:(r + 1) * 128, i * 128:(i + 1) * 128], o_sem.at[r, i])
            c.start()
            writes.append(c)
    for c in writes + carried:
        c.wait()


def local(self_q, self_k, self_v, doc_ids, cross_q, image_keys, image_values, image_list, image_lengths, cross_mask):
    bf16, f32, i32 = jnp.bfloat16, jnp.float32, jnp.int32
    hbm = pl.BlockSpec(memory_space=pltpu.HBM)
    dma = lambda *shape: pltpu.SemaphoreType.DMA(shape)
    place = lambda x: pltpu.with_memory_space_constraint(x, pltpu.HBM)
    kv, attended = pl.pallas_call(
        exchange,
        name="exchange",
        out_shape=(pltpu.HBM((32, 4, 2, 128, 256), bf16), pltpu.HBM((256, 2048), bf16)),
        in_specs=[hbm] * 6,
        out_specs=(hbm, hbm),
        scratch_shapes=[
            pltpu.VMEM((4096, 128), bf16), pltpu.VMEM((4096, 128), bf16),
            pltpu.VMEM((1280, 256), bf16), pltpu.VMEM((1280, 256), bf16),
            pltpu.VMEM((1, 2048), i32), pltpu.VMEM((256, 1280), f32),
            pltpu.VMEM((4096, 128), f32), pltpu.VMEM((4096, 128), f32), pltpu.VMEM((4096, 128), f32),
            dma(3, 4, 2), dma(3, 4, 2), dma(4, 2), dma(3, 4), dma(3, 4), dma(4, 3, 4), dma(4, 3, 4),
            dma(4, 4, 4), dma(4, 4, 4), dma(6, 2), dma(6, 2), dma(19), dma(16),
        ],
        compiler_params=pltpu.CompilerParams(collective_id=0, has_side_effects=True, vmem_limit_bytes=48 << 20),
    )(*(place(x) for x in (image_keys, image_values, self_k[0], self_v[0], doc_ids, self_q[0])))
    cross_out, self_out = pl.pallas_call(
        cross_kernel,
        name="cross_attend",
        out_shape=(pltpu.HBM((256, 2048), bf16), pltpu.HBM((256, 2048), bf16)),
        in_specs=[hbm] * 6,
        out_specs=(hbm, hbm),
        scratch_shapes=[
            pltpu.SMEM((4, 8, 32), i32), pltpu.SMEM((128,), i32), pltpu.SMEM((1, 2, 32), i32),
            pltpu.VMEM((4096, 128), bf16), pltpu.VMEM((4096, 128), bf16), pltpu.VMEM((2, 2, 4096, 256), bf16),
            pltpu.VMEM((2048, 128), f32), pltpu.VMEM((2048, 128), f32), pltpu.VMEM((2048, 128), f32),
            dma(3), dma(2, 16), dma(2, 16), dma(2), dma(4),
        ],
        compiler_params=pltpu.CompilerParams(vmem_limit_bytes=48 << 20),
    )(*(place(x) for x in (image_list, image_lengths, cross_mask, cross_q[0])), place(kv), place(attended))
    return self_out[None], cross_out[None]


def solution(mesh):
    in_specs = (
        P("enc", "seq", "mp"),
        P("enc", "seq", "mp"),
        P("enc", "seq", "mp"),
        P("enc", None),
        P("enc", "seq", "mp"),
        P(("seq", "enc"), "mp", None),
        P(("seq", "enc"), "mp", None),
        P(),
        P(),
        P("enc", "seq", None),
    )
    out_specs = (P("enc", "seq", "mp"), P("enc", "seq", "mp"))
    return jax.shard_map(local, mesh=mesh, in_specs=in_specs, out_specs=out_specs, check_vma=False)
```

```python
import functools
import jax
import jax.numpy as jnp
from jax import lax
from jax.experimental import pallas as pl
from jax.experimental.pallas import tpu as pltpu
from jax.sharding import PartitionSpec as P

HD = 128
NEG = -1e30
START = -5e29
LOG2E = 1.4426950408889634
FACTOR = HD ** (-0.5) * LOG2E
MESH = pl.DeviceIdType.MESH
TILE = 32
CHUNK = 512
NT = (((1,), (1,)), ((), ()))


def softmax_step(sc, m_ref, l_ref, a_ref, v, rows):
    n = sc.shape[1] // 128
    m_old = m_ref[rows, :]
    m_new = jnp.maximum(m_old, jnp.max(sc, axis=1, keepdims=True))
    p = jnp.exp2((sc - jnp.concatenate([m_new] * n, axis=1)) * FACTOR)
    alpha = jnp.exp2((m_old - m_new) * FACTOR)
    part = p[:, 0:128]
    for i in range(1, n):
        part = part + p[:, i * 128:(i + 1) * 128]
    l_ref[rows, :] = l_ref[rows, :] * alpha + part
    a_ref[rows, :] = a_ref[rows, :] * alpha + jnp.dot(p.astype(jnp.bfloat16), v, preferred_element_type=jnp.float32)
    m_ref[rows, :] = m_new


def clear(m_ref, l_ref, a_ref):
    m_ref[...] = jnp.full_like(m_ref, START)
    l_ref[...] = jnp.zeros_like(l_ref)
    a_ref[...] = jnp.zeros_like(a_ref)


def exchange(
    ik, iv, sk, sv, ids, sq, kv, self_out, qs, os, own, kbuf, vbuf, docs, bias, m_ref, l_ref, a_ref,
    mp_s, mp_r, own_s, r1_s, r1_r, r2_s, r2_r, sib_s, sib_r, tx_s, tx_r, load_sem, out_sem,
):
    s = lax.axis_index("seq")
    g = lax.axis_index("mp")
    e = lax.axis_index("enc")
    core = lax.rem(s, 2)
    y = s // 2
    sibling = (s + 1 - 2 * core, g, e)
    me = s * 4 + e

    def place(c):
        return e + c * (y - e), y + c * (e - y)

    p1, p2 = place(core)
    up = lambda p: lax.rem(p + 1, 4)
    down = lambda p: lax.rem(p + 3, 4)
    steps = (lambda p: p, down, up, lambda p: lax.rem(p + 2, 4))

    def at(q1, q2):
        return (2 * (q2 + core * (q1 - q2)) + core, g, q1 + core * (q2 - q1))

    def piece(i1, i2, c=core):
        q1, q2 = place(c)
        return (1 + 7 * c) * steps[i1](q1) + (8 - 7 * c) * steps[i2](q2) + 4 * c

    right1, left1 = at(up(p1), p2), at(down(p1), p2)
    right2, left2 = at(p1, up(p2)), at(p1, down(p2))

    loads = [
        pltpu.make_async_copy(ids, docs, load_sem.at[0]),
        pltpu.make_async_copy(sk, kbuf.at[0:256, :], load_sem.at[1]),
        pltpu.make_async_copy(sv, vbuf.at[0:256, :], load_sem.at[2]),
    ]
    own_cols = pl.ds(pl.multiple_of(g * 256, 256), 256)
    bring = [
        pltpu.make_async_copy(src.at[:, :, own_cols], own.at[half], load_sem.at[19 + half]) for half, src in ((0, ik), (1, iv))
    ]
    for i in range(16):
        loads.append(pltpu.make_async_copy(sq.at[:, i * 128:(i + 1) * 128], qs.at[i * 256:(i + 1) * 256, :], load_sem.at[3 + i]))

    barrier = pltpu.get_barrier_semaphore()
    greet = [right1, left1, right2, left2, sibling] + [(s, lax.rem(g + d, 4), e) for d in (1, 2, 3)]
    for who in greet:
        pl.semaphore_signal(barrier, inc=1, device_id=who, device_id_type=MESH)
    for c in bring + loads:
        c.start()
    pl.semaphore_wait(barrier, len(greet))

    def remote(src, dst, ss, rs, who):
        return pltpu.make_async_remote_copy(
            src_ref=src, dst_ref=dst, send_sem=ss, recv_sem=rs, device_id=who, device_id_type=MESH
        )

    sends = []

    def go(h, c, ss, rs, who):
        r = remote(kv.at[h, c], kv.at[h, c], ss, rs, who)
        r.start()
        sends.append(r)

    def landed(h, c, rs):
        pltpu.make_async_copy(kv.at[h, c], kv.at[h, c], rs).wait()

    mine = pl.ds(pl.multiple_of(g * TILE, TILE), TILE)
    first = []
    for c in range(4):
        group = []
        for d in (1, 2, 3):
            to = lax.rem(g + d, 4)
            cols = pl.ds(pl.multiple_of(to * 256, 256), 256)
            for half, src in ((0, ik), (1, iv)):
                a, b = src.at[c, :, cols], kv.at[me, c, half, mine, :]
                r = remote(a, b, mp_s.at[d - 1, c, half], mp_r.at[d - 1, c, half], (s, to, e))
                r.start()
                group.append(r)
        first.append(group)
    for r in bring:
        r.wait()
    for c in range(4):
        r = pltpu.make_async_copy(own.at[:, c], kv.at[me, c, :, mine, :], own_s.at[c])
        r.start()
        first[c].append(r)

    text = []

    def guarded(cond, r):
        text.append((cond, r))

        @pl.when(cond)
        def _():
            r.start()

    def text_at(buf, d):
        return buf.at[256 * d:256 * (d + 1), :]

    def text_landed(cond, d, half, sem):
        @pl.when(cond)
        def _():
            ref = text_at((kbuf, vbuf)[half], d)
            pltpu.make_async_copy(ref, ref, sem).wait()

    ahead = (lax.rem(s + 2, 8), g, e)
    for half, src in ((0, sk), (1, sv)):
        buf = (kbuf, vbuf)[half]
        guarded(s + 2 < 8, remote(src, text_at(buf, 2), tx_s.at[0, half], tx_r.at[0, half], ahead))
        guarded(core == 0, remote(src, text_at(buf, 1), tx_s.at[1, half], tx_r.at[1, half], sibling))
    for d in range(1, 5):
        @pl.when(s < d)
        def _():
            for buf in (kbuf, vbuf):
                buf[256 * d:256 * (d + 1), :] = jnp.zeros((256, 256), jnp.bfloat16)

    def text_onward():
        for half in (0, 1):
            buf = (kbuf, vbuf)[half]
            text_landed(s >= 2, 2, half, tx_r.at[0, half])
            got = text_at(buf, 2)
            guarded((s >= 2) & (s + 2 < 8), remote(got, text_at(buf, 4), tx_s.at[4, half], tx_r.at[4, half], ahead))
            guarded((s >= 2) & (core == 0), remote(got, text_at(buf, 3), tx_s.at[2, half], tx_r.at[2, half], sibling))
            guarded((s >= 2) & (core == 1), remote(got, text_at(buf, 1), tx_s.at[3, half], tx_r.at[3, half], sibling))

    def text_near():
        for half in (0, 1):
            text_landed(core == 1, 1, half, tx_r.at[1, half])
            text_landed((s >= 2) & (core == 0), 1, half, tx_r.at[3, half])

    def text_far():
        for half in (0, 1):
            buf = (kbuf, vbuf)[half]
            text_landed(s >= 4, 4, half, tx_r.at[4, half])
            guarded((s >= 4) & (core == 1), remote(text_at(buf, 4), text_at(buf, 3), tx_s.at[5, half], tx_r.at[5, half], sibling))
        for half in (0, 1):
            text_landed((s >= 2) & (core == 1), 3, half, tx_r.at[2, half])
            text_landed((s >= 4) & (core == 0), 3, half, tx_r.at[5, half])

    def to_sibling(i1, i2, c):
        go(piece(i1, i2), c, sib_s.at[i1, i2, c], sib_r.at[i1, i2, c], sibling)

    def ring1(c):
        h = piece(0, 0)
        go(h, c, r1_s.at[0, c], r1_r.at[0, c], right1)
        go(h, c, r1_s.at[1, c], r1_r.at[1, c], left1)

    def ring2(i1, c):
        h = piece(i1, 0)
        go(h, c, r2_s.at[i1, 0, c], r2_r.at[i1, 0, c], right2)
        go(h, c, r2_s.at[i1, 1, c], r2_r.at[i1, 1, c], left2)

    def onward1(c):
        for i1, far, to in ((1, c < 2, right1), (2, c >= 2, left1)):
            landed(piece(i1, 0), c, r1_r.at[i1 - 1, c])
            if far:
                go(piece(i1, 0), c, r1_s.at[2, c], r1_r.at[2, c], to)
            ring2(i1, c)
            to_sibling(i1, 0, c)

    def onward2(i1, c):
        for i2, far, to in ((1, c < 1, right2), (2, c >= 1, left2)):
            landed(piece(i1, i2), c, r2_r.at[i1, i2 - 1, c])
            if far:
                go(piece(i1, i2), c, r2_s.at[i1, 2, c], r2_r.at[i1, 2, c], to)
            to_sibling(i1, i2, c)

    def self_setup():
        for c in loads:
            c.wait()

        def row_docs(block):
            return docs[:, pl.ds(pl.multiple_of(block * 256, 256), 256)].astype(jnp.float32)

        own = row_docs(s)
        column = jnp.concatenate(
            [jnp.transpose(jnp.broadcast_to(own[:, i * 128:(i + 1) * 128], (128, 128))) for i in (0, 1)], axis=0
        )
        column = jnp.concatenate([column, column], axis=1)
        rows = lax.broadcasted_iota(jnp.int32, (256, 256), 0)
        cols = lax.broadcasted_iota(jnp.int32, (256, 256), 1)
        bias[:, 0:256] = jnp.where((column == own) & (cols <= rows), 0.0, NEG)
        for d in range(1, 5):
            seen = (column == row_docs(jnp.maximum(s - d, 0))) & (rows - rows + s >= d)
            bias[:, d * 256:(d + 1) * 256] = jnp.where(seen, 0.0, NEG)

    def self_units(lo, hi, key, size):
        def unit(q, carry):
            cols = pl.ds(pl.multiple_of(q // 2 * 128, 128), 128)
            rows = pl.ds(pl.multiple_of(q * 1024, 1024), 1024)
            sc = lax.dot_general(qs[rows, :], kbuf[key:key + size, cols], NT, preferred_element_type=jnp.float32)
            sc = sc + jnp.concatenate([bias[:, key:key + size]] * 4, axis=0)
            softmax_step(sc, m_ref, l_ref, a_ref, vbuf[key:key + size, cols], rows)
            return carry

        lax.fori_loop(lo, hi, unit, 0)

    writes = []

    def emit():
        for i in range(16):
            rows = slice(i * 256, (i + 1) * 256)
            total = jnp.sum(l_ref[rows, :], axis=1, keepdims=True)
            os[rows, :] = (a_ref[rows, :] / jnp.maximum(total, 1.0)).astype(jnp.bfloat16)
            c = pltpu.make_async_copy(os.at[rows, :], self_out.at[:, i * 128:(i + 1) * 128], out_sem.at[i])
            c.start()
            writes.append(c)

    for c in range(4):
        for r in first[c]:
            r.wait()
        ring1(c)
        ring2(0, c)
        to_sibling(0, 0, c)
    self_setup()
    clear(m_ref, l_ref, a_ref)
    text_onward()
    onward1(0)
    onward2(0, 0)
    text_near()
    self_units(0, 1, 0, 512)
    onward1(1)
    onward2(0, 1)
    self_units(1, 2, 0, 512)
    onward1(2)
    onward2(0, 2)
    self_units(2, 3, 0, 512)
    onward1(3)
    onward2(0, 3)
    self_units(3, 4, 0, 512)
    text_far()
    for c in range(4):
        landed(piece(3, 0), c, r1_r.at[2, c])
        ring2(3, c)
        to_sibling(3, 0, c)
        for i1 in (1, 2):
            onward2(i1, c)
        self_units(c, c + 1, 512, 512)
    for c in range(4):
        onward2(3, c)
        self_units(c, c + 1, 1024, 256)
    emit()
    for i1 in range(4):
        for c in range(4):
            landed(piece(i1, 3), c, r2_r.at[i1, 2, c])
            to_sibling(i1, 3, c)

    for i1 in range(4):
        for i2 in range(4):
            for c in range(4):
                landed(piece(i1, i2, 1 - core), c, sib_r.at[i1, i2, c])
    for r in sends:
        r.wait_send()
    for cond, r in text:
        @pl.when(cond)
        def _():
            r.wait_send()
    for c in writes:
        c.wait()


def cross_kernel(lists, lengths, flags, q_ref, kv_ref, done, out_ref, self_ref, list_ref, len_ref, mask_ref, qs, os, buf, through, m_ref, l_ref, a_ref, t_sem, q_sem, o_sem, kv_sem, d_sem):
    s = lax.axis_index("seq")
    e = lax.axis_index("enc")
    per = CHUNK // TILE
    tables = [
        pltpu.make_async_copy(lists, list_ref, t_sem.at[0]),
        pltpu.make_async_copy(lengths, len_ref, t_sem.at[1]),
        pltpu.make_async_copy(flags, mask_ref, t_sem.at[2]),
    ]
    reads = [
        pltpu.make_async_copy(
            q_ref.at[r * 128:(r + 1) * 128, i * 128:(i + 1) * 128],
            qs.at[r * 2048 + i * 128:r * 2048 + (i + 1) * 128, :], q_sem.at[r, i],
        )
        for r in range(2) for i in range(16)
    ]
    carried = [
        pltpu.make_async_copy(a.at[i * 64:(i + 1) * 64, :], b.at[i * 64:(i + 1) * 64, :], d_sem.at[way, i])
        for way, (a, b) in enumerate(((done, through), (through, self_ref))) for i in range(4)
    ]
    for c in tables + reads + carried[:4]:
        c.start()
    for c in tables:
        c.wait()

    def fetch(r):
        def slot(k, pos):
            img = list_ref[e, s, k]
            n = jnp.where(mask_ref[0, r, k] == 1, len_ref[img] // TILE, 0)
            for size in range(1, 5):
                @pl.when(n == size)
                def _():
                    pltpu.make_async_copy(
                        kv_ref.at[img // 4, lax.rem(img, 4), :, 0:size * TILE, :],
                        buf.at[r, :, pl.ds(pl.multiple_of(pos * TILE, TILE), size * TILE), :], kv_sem.at[r],
                    ).start()
            return pos + n

        return lax.fori_loop(0, 32, slot, 0)

    counts = [fetch(0), fetch(1)]
    writes = []
    for r in range(2):
        n = counts[r]
        clear(m_ref, l_ref, a_ref)
        if r == 0:
            for c in reads + carried[:4]:
                c.wait()
            for c in carried[4:]:
                c.start()

        def arrived(p, carry):
            ref = buf.at[r, :, 0:TILE, :]
            pltpu.make_async_copy(ref, ref, kv_sem.at[r]).wait()
            return carry

        lax.fori_loop(0, n, arrived, 0)

        def blank(p, carry):
            buf[r, 1, pl.ds(pl.multiple_of(p * TILE, TILE), TILE), :] = jnp.zeros((TILE, 256), jnp.bfloat16)
            return carry

        lax.fori_loop(n, (n + 7) // 8 * 8, blank, 0)

        def chunk(c, size, masked):
            at = pl.ds(pl.multiple_of(c * CHUNK, CHUNK), size)
            for j in range(2):
                cols = slice(j * 128, (j + 1) * 128)
                rows = slice(j * 1024, (j + 1) * 1024)
                sc = lax.dot_general(
                    qs[r * 2048 + j * 1024:r * 2048 + (j + 1) * 1024, :], buf[r, 0, at, cols], NT,
                    preferred_element_type=jnp.float32,
                )
                if masked:
                    keys = lax.broadcasted_iota(jnp.int32, sc.shape, 1)
                    sc = jnp.where(keys < n * TILE - c * CHUNK, sc, NEG)
                softmax_step(sc, m_ref, l_ref, a_ref, buf[r, 1, at, cols], rows)

        full = n // per
        left = n - full * per

        def body(c, carry):
            chunk(c, CHUNK, False)
            return carry

        lax.fori_loop(0, full, body, 0)

        @pl.when(left > per // 2)
        def _():
            chunk(full, CHUNK, True)

        @pl.when((left > 0) & (left <= per // 2))
        def _():
            chunk(full, CHUNK // 2, True)

        for i in range(16):
            rows = slice(i * 128, (i + 1) * 128)
            to = slice(r * 2048 + i * 128, r * 2048 + (i + 1) * 128)
            total = jnp.sum(l_ref[rows, :], axis=1, keepdims=True)
            os[to, :] = (a_ref[rows, :] / jnp.maximum(total, 1.0)).astype(jnp.bfloat16)
            c = pltpu.make_async_copy(os.at[to, :], out_ref.at[r * 128:(r + 1) * 128, i * 128:(i + 1) * 128], o_sem.at[r, i])
            c.start()
            writes.append(c)
    for c in writes + carried[4:]:
        c.wait()


def local(self_q, self_k, self_v, doc_ids, cross_q, image_keys, image_values, image_list, image_lengths, cross_mask):
    bf16, f32, i32 = jnp.bfloat16, jnp.float32, jnp.int32
    hbm = pl.BlockSpec(memory_space=pltpu.HBM)
    dma = lambda *shape: pltpu.SemaphoreType.DMA(shape)
    place = lambda x: pltpu.with_memory_space_constraint(x, pltpu.HBM)
    kv, attended = pl.pallas_call(
        exchange,
        name="exchange",
        out_shape=(pltpu.HBM((32, 4, 2, 128, 256), bf16), pltpu.HBM((256, 2048), bf16)),
        in_specs=[hbm] * 6,
        out_specs=(hbm, hbm),
        scratch_shapes=[
            pltpu.VMEM((4096, 128), bf16), pltpu.VMEM((4096, 128), bf16), pltpu.VMEM((2, 4, TILE, 256), bf16),
            pltpu.VMEM((1280, 256), bf16), pltpu.VMEM((1280, 256), bf16),
            pltpu.VMEM((1, 2048), i32), pltpu.VMEM((256, 1280), f32),
            pltpu.VMEM((4096, 128), f32), pltpu.VMEM((4096, 128), f32), pltpu.VMEM((4096, 128), f32),
            dma(3, 4, 2), dma(3, 4, 2), dma(4), dma(3, 4), dma(3, 4), dma(4, 3, 4), dma(4, 3, 4),
            dma(4, 4, 4), dma(4, 4, 4), dma(6, 2), dma(6, 2), dma(21), dma(16),
        ],
        compiler_params=pltpu.CompilerParams(collective_id=0, has_side_effects=True, vmem_limit_bytes=48 << 20),
    )(*(place(x) for x in (image_keys, image_values, self_k[0], self_v[0], doc_ids, self_q[0])))
    cross_out, self_out = pl.pallas_call(
        cross_kernel,
        name="cross_attend",
        out_shape=(pltpu.HBM((256, 2048), bf16), pltpu.HBM((256, 2048), bf16)),
        in_specs=[hbm] * 6,
        out_specs=(hbm, hbm),
        scratch_shapes=[
            pltpu.SMEM((4, 8, 32), i32), pltpu.SMEM((128,), i32), pltpu.SMEM((1, 2, 32), i32),
            pltpu.VMEM((4096, 128), bf16), pltpu.VMEM((4096, 128), bf16), pltpu.VMEM((2, 2, 4096, 256), bf16), pltpu.VMEM((256, 2048), bf16),
            pltpu.VMEM((2048, 128), f32), pltpu.VMEM((2048, 128), f32), pltpu.VMEM((2048, 128), f32),
            dma(3), dma(2, 16), dma(2, 16), dma(2), dma(2, 4),
        ],
        compiler_params=pltpu.CompilerParams(vmem_limit_bytes=48 << 20),
    )(*(place(x) for x in (image_list, image_lengths, cross_mask, cross_q[0])), place(kv), place(attended))
    return self_out[None], cross_out[None]


def solution(mesh):
    in_specs = (
        P("enc", "seq", "mp"),
        P("enc", "seq", "mp"),
        P("enc", "seq", "mp"),
        P("enc", None),
        P("enc", "seq", "mp"),
        P(("seq", "enc"), "mp", None),
        P(("seq", "enc"), "mp", None),
        P(),
        P(),
        P("enc", "seq", None),
    )
    out_specs = (P("enc", "seq", "mp"), P("enc", "seq", "mp"))
    return jax.shard_map(local, mesh=mesh, in_specs=in_specs, out_specs=out_specs, check_vma=False)
```

```python
import functools
import jax
import jax.numpy as jnp
from jax import lax
from jax.experimental import pallas as pl
from jax.experimental.pallas import tpu as pltpu
from jax.sharding import PartitionSpec as P

HD = 128
NEG = -1e30
START = -5e29
LOG2E = 1.4426950408889634
FACTOR = HD ** (-0.5) * LOG2E
MESH = pl.DeviceIdType.MESH
TILE = 32
CHUNK = 512
NT = (((1,), (1,)), ((), ()))


def softmax_step(sc, m_ref, l_ref, a_ref, v, rows):
    n = sc.shape[1] // 128
    m_old = m_ref[rows, :]
    m_new = jnp.maximum(m_old, jnp.max(sc, axis=1, keepdims=True))
    p = jnp.exp2((sc - jnp.concatenate([m_new] * n, axis=1)) * FACTOR)
    alpha = jnp.exp2((m_old - m_new) * FACTOR)
    part = p[:, 0:128]
    for i in range(1, n):
        part = part + p[:, i * 128:(i + 1) * 128]
    l_ref[rows, :] = l_ref[rows, :] * alpha + part
    a_ref[rows, :] = a_ref[rows, :] * alpha + jnp.dot(p.astype(jnp.bfloat16), v, preferred_element_type=jnp.float32)
    m_ref[rows, :] = m_new


def clear(m_ref, l_ref, a_ref):
    m_ref[...] = jnp.full_like(m_ref, START)
    l_ref[...] = jnp.zeros_like(l_ref)
    a_ref[...] = jnp.zeros_like(a_ref)


def exchange(
    ik, iv, sk, sv, ids, sq, kv, self_out, qs, os, own, kbuf, vbuf, docs, bias, m_ref, l_ref, a_ref,
    mp_s, mp_r, own_s, r1_s, r1_r, r2_s, r2_r, sib_s, sib_r, tx_s, tx_r, load_sem, out_sem,
):
    s = lax.axis_index("seq")
    g = lax.axis_index("mp")
    e = lax.axis_index("enc")
    core = lax.rem(s, 2)
    y = s // 2
    sibling = (s + 1 - 2 * core, g, e)
    me = s * 4 + e

    def place(order):
        return e + order * (y - e), y + order * (e - y)

    steps = (lambda p: p, lambda p: lax.rem(p + 3, 4), lambda p: lax.rem(p + 1, 4), lambda p: lax.rem(p + 2, 4))

    def spot(i1, i2, order):
        p1, p2 = place(order)
        q1, q2 = steps[i1](p1), steps[i2](p2)
        return q2 + order * (q1 - q2), q1 + order * (q2 - q1)

    def at(i1, i2, order):
        yy, zz = spot(i1, i2, order)
        return (2 * yy + core, g, zz)

    def piece(i1, i2, order, of=core):
        yy, zz = spot(i1, i2, order)
        return (2 * yy + of) * 4 + zz

    turn = (g, lax.rem(g + 3, 4), lax.rem(g + 1, 4), lax.rem(g + 2, 4))
    chunks = (
        (turn[0], slice(0, 4), core), (turn[1], slice(0, 4), core), (turn[2], slice(0, 4), core),
        (turn[3], slice(0, 2), core), (turn[3], slice(2, 4), 1),
    )

    loads = [
        pltpu.make_async_copy(ids, docs, load_sem.at[0]),
        pltpu.make_async_copy(sk, kbuf.at[0:256, :], load_sem.at[1]),
        pltpu.make_async_copy(sv, vbuf.at[0:256, :], load_sem.at[2]),
    ]
    own_cols = pl.ds(pl.multiple_of(g * 256, 256), 256)
    bring = [
        pltpu.make_async_copy(src.at[:, :, own_cols], own.at[:, half], load_sem.at[19 + half]) for half, src in ((0, ik), (1, iv))
    ]
    for i in range(16):
        loads.append(pltpu.make_async_copy(sq.at[:, i * 128:(i + 1) * 128], qs.at[i * 256:(i + 1) * 256, :], load_sem.at[3 + i]))

    barrier = pltpu.get_barrier_semaphore()
    greet = [at(2, 0, core), at(1, 0, core), at(0, 2, core), at(0, 1, core), sibling] + [(s, lax.rem(g + d, 4), e) for d in (1, 2, 3)]
    for who in greet:
        pl.semaphore_signal(barrier, inc=1, device_id=who, device_id_type=MESH)
    for c in bring + loads:
        c.start()
    pl.semaphore_wait(barrier, len(greet))

    def remote(src, dst, ss, rs, who):
        return pltpu.make_async_remote_copy(
            src_ref=src, dst_ref=dst, send_sem=ss, recv_sem=rs, device_id=who, device_id_type=MESH
        )

    sends = []

    def go(src, dst, ss, rs, who, cond=None):
        r = remote(src, dst, ss, rs, who)
        sends.append((cond, r))
        if cond is None:
            r.start()
        else:
            @pl.when(cond)
            def _():
                r.start()

    def block(h, c):
        return kv.at[h, chunks[c][0], chunks[c][1]]

    def landed(h, c, rs):
        pltpu.make_async_copy(block(h, c), block(h, c), rs).wait()

    arriving = {}
    for d in (1, 3, 2):
        to = lax.rem(g + d, 4)
        cols = pl.ds(pl.multiple_of(to * 256, 256), 256)
        for half, src in ((0, ik), (1, iv)):
            r = remote(src.at[:, :, cols], kv.at[me, g, :, half], mp_s.at[d - 1, half], mp_r.at[d - 1, half], (s, to, e))
            r.start()
            arriving[d, half] = r

    text = []

    def guarded(cond, r):
        text.append((cond, r))

        @pl.when(cond)
        def _():
            r.start()

    def text_at(buf, d):
        return buf.at[256 * d:256 * (d + 1), :]

    def text_landed(cond, d, half, sem):
        @pl.when(cond)
        def _():
            ref = text_at((kbuf, vbuf)[half], d)
            pltpu.make_async_copy(ref, ref, sem).wait()

    ahead = (lax.rem(s + 2, 8), g, e)
    for half, src in ((0, sk), (1, sv)):
        buf = (kbuf, vbuf)[half]
        guarded(s + 2 < 8, remote(src, text_at(buf, 2), tx_s.at[0, half], tx_r.at[0, half], ahead))
        guarded(core == 0, remote(src, text_at(buf, 1), tx_s.at[1, half], tx_r.at[1, half], sibling))
    for d in range(1, 5):
        @pl.when(s < d)
        def _():
            for buf in (kbuf, vbuf):
                buf[256 * d:256 * (d + 1), :] = jnp.zeros((256, 256), jnp.bfloat16)

    def text_onward():
        for half in (0, 1):
            buf = (kbuf, vbuf)[half]
            text_landed(s >= 2, 2, half, tx_r.at[0, half])
            got = text_at(buf, 2)
            guarded((s >= 2) & (s + 2 < 8), remote(got, text_at(buf, 4), tx_s.at[4, half], tx_r.at[4, half], ahead))
            guarded((s >= 2) & (core == 0), remote(got, text_at(buf, 3), tx_s.at[2, half], tx_r.at[2, half], sibling))
            guarded((s >= 2) & (core == 1), remote(got, text_at(buf, 1), tx_s.at[3, half], tx_r.at[3, half], sibling))

    def text_near():
        for half in (0, 1):
            text_landed(core == 1, 1, half, tx_r.at[1, half])
            text_landed((s >= 2) & (core == 0), 1, half, tx_r.at[3, half])

    def text_far():
        for half in (0, 1):
            buf = (kbuf, vbuf)[half]
            text_landed(s >= 4, 4, half, tx_r.at[4, half])
            guarded((s >= 4) & (core == 1), remote(text_at(buf, 4), text_at(buf, 3), tx_s.at[5, half], tx_r.at[5, half], sibling))
        for half in (0, 1):
            text_landed((s >= 2) & (core == 1), 3, half, tx_r.at[2, half])
            text_landed((s >= 4) & (core == 0), 3, half, tx_r.at[5, half])

    def to_sibling(i1, i2, c, src=None):
        ref = block(piece(i1, i2, chunks[c][2]), c)
        go(ref if src is None else src, ref, sib_s.at[i1, i2, c], sib_r.at[i1, i2, c], sibling)

    def ring1(c, src=None):
        order = chunks[c][2]
        ref = block(me, c)
        go(ref if src is None else src, ref, r1_s.at[0, c], r1_r.at[0, c], at(2, 0, order))
        go(ref if src is None else src, ref, r1_s.at[1, c], r1_r.at[1, c], at(1, 0, order))

    def ring2(i1, c, src=None):
        order = chunks[c][2]
        ref = block(piece(i1, 0, order), c)
        go(ref if src is None else src, ref, r2_s.at[i1, 0, c], r2_r.at[i1, 0, c], at(0, 2, order))
        go(ref if src is None else src, ref, r2_s.at[i1, 1, c], r2_r.at[i1, 1, c], at(0, 1, order))

    def release(c, src=None):
        ring1(c, src)
        ring2(0, c, src)
        to_sibling(0, 0, c, src)

    def onward1(c):
        order = chunks[c][2]
        for i1, far, to in ((1, c < 2, at(2, 0, order)), (2, c >= 2, at(1, 0, order))):
            h = piece(i1, 0, order)
            landed(h, c, r1_r.at[i1 - 1, c])
            if far:
                go(block(h, c), block(h, c), r1_s.at[2, c], r1_r.at[2, c], to)
            ring2(i1, c)
            to_sibling(i1, 0, c)

    def onward2(i1, c):
        order = chunks[c][2]
        far = {0: (True, False), 1: (core == 1, core == 0)}.get(c, (False, True))
        for i2, cond, to in ((1, far[0], at(0, 2, order)), (2, far[1], at(0, 1, order))):
            h = piece(i1, i2, order)
            landed(h, c, r2_r.at[i1, i2 - 1, c])
            if cond is not False:
                go(block(h, c), block(h, c), r2_s.at[i1, 2, c], r2_r.at[i1, 2, c], to, None if cond is True else cond)
            to_sibling(i1, i2, c)

    def across1(c):
        landed(piece(3, 0, chunks[c][2]), c, r1_r.at[2, c])
        ring2(3, c)
        to_sibling(3, 0, c)

    def across2(i1, c):
        landed(piece(i1, 3, chunks[c][2]), c, r2_r.at[i1, 2, c])
        to_sibling(i1, 3, c)

    def self_setup():
        for c in loads:
            c.wait()

        def row_docs(block):
            return docs[:, pl.ds(pl.multiple_of(block * 256, 256), 256)].astype(jnp.float32)

        own = row_docs(s)
        column = jnp.concatenate(
            [jnp.transpose(jnp.broadcast_to(own[:, i * 128:(i + 1) * 128], (128, 128))) for i in (0, 1)], axis=0
        )
        column = jnp.concatenate([column, column], axis=1)
        rows = lax.broadcasted_iota(jnp.int32, (256, 256), 0)
        cols = lax.broadcasted_iota(jnp.int32, (256, 256), 1)
        bias[:, 0:256] = jnp.where((column == own) & (cols <= rows), 0.0, NEG)
        for d in range(1, 5):
            seen = (column == row_docs(jnp.maximum(s - d, 0))) & (rows - rows + s >= d)
            bias[:, d * 256:(d + 1) * 256] = jnp.where(seen, 0.0, NEG)

    def self_units(lo, hi, key, size):
        def unit(q, carry):
            cols = pl.ds(pl.multiple_of(q // 2 * 128, 128), 128)
            rows = pl.ds(pl.multiple_of(q * 1024, 1024), 1024)
            sc = lax.dot_general(qs[rows, :], kbuf[key:key + size, cols], NT, preferred_element_type=jnp.float32)
            sc = sc + jnp.concatenate([bias[:, key:key + size]] * 4, axis=0)
            softmax_step(sc, m_ref, l_ref, a_ref, vbuf[key:key + size, cols], rows)
            return carry

        lax.fori_loop(lo, hi, unit, 0)

    writes = []

    def emit():
        for i in range(16):
            rows = slice(i * 256, (i + 1) * 256)
            total = jnp.sum(l_ref[rows, :], axis=1, keepdims=True)
            os[rows, :] = (a_ref[rows, :] / jnp.maximum(total, 1.0)).astype(jnp.bfloat16)
            c = pltpu.make_async_copy(os.at[rows, :], self_out.at[:, i * 128:(i + 1) * 128], out_sem.at[i])
            c.start()
            writes.append(c)

    for r in bring:
        r.wait()
    keep = pltpu.make_async_copy(own, kv.at[me, g], own_s.at[0])
    keep.start()
    release(0, own)
    self_setup()
    clear(m_ref, l_ref, a_ref)
    for c, d in ((1, 1), (2, 3), (3, 2)):
        for half in (0, 1):
            arriving[d, half].wait_recv()
        release(c)
    release(4)
    text_onward()
    onward1(0)
    onward2(0, 0)
    text_near()
    self_units(0, 1, 0, 512)
    onward1(1)
    onward2(0, 1)
    self_units(1, 2, 0, 512)
    onward1(2)
    onward2(0, 2)
    self_units(2, 3, 0, 512)
    onward1(3)
    onward2(0, 3)
    onward1(4)
    onward2(0, 4)
    self_units(3, 4, 0, 512)
    text_far()
    for c in range(5):
        across1(c)
        for i1 in (1, 2):
            onward2(i1, c)
        if c < 4:
            self_units(c, c + 1, 512, 512)
    for c in range(5):
        onward2(3, c)
        if c < 4:
            self_units(c, c + 1, 1024, 256)
    emit()
    for i1 in range(4):
        for c in range(5):
            across2(i1, c)

    for i1 in range(4):
        for i2 in range(4):
            for c in range(5):
                order = 1 - core if c < 4 else 1
                landed(piece(i1, i2, order, 1 - core), c, sib_r.at[i1, i2, c])
    for cond, r in sends + text:
        if cond is None:
            r.wait_send()
        else:
            @pl.when(cond)
            def _():
                r.wait_send()
    keep.wait()
    for r in arriving.values():
        r.wait_send()
    for c in writes:
        c.wait()


def cross_kernel(lists, lengths, flags, q_ref, kv_ref, done, out_ref, self_ref, list_ref, len_ref, mask_ref, qs, os, buf, through, m_ref, l_ref, a_ref, t_sem, q_sem, o_sem, kv_sem, d_sem):
    s = lax.axis_index("seq")
    e = lax.axis_index("enc")
    per = CHUNK // TILE
    tables = [
        pltpu.make_async_copy(lists, list_ref, t_sem.at[0]),
        pltpu.make_async_copy(lengths, len_ref, t_sem.at[1]),
        pltpu.make_async_copy(flags, mask_ref, t_sem.at[2]),
    ]
    reads = [
        pltpu.make_async_copy(
            q_ref.at[r * 128:(r + 1) * 128, i * 128:(i + 1) * 128],
            qs.at[r * 2048 + i * 128:r * 2048 + (i + 1) * 128, :], q_sem.at[r, i],
        )
        for r in range(2) for i in range(16)
    ]
    carried = [
        pltpu.make_async_copy(a.at[i * 64:(i + 1) * 64, :], b.at[i * 64:(i + 1) * 64, :], d_sem.at[way, i])
        for way, (a, b) in enumerate(((done, through), (through, self_ref))) for i in range(4)
    ]
    for c in tables + reads + carried[:4]:
        c.start()
    for c in tables:
        c.wait()

    def fetch(r):
        def slot(k, pos):
            img = list_ref[e, s, k]
            n = jnp.where(mask_ref[0, r, k] == 1, len_ref[img] // TILE, 0)
            for size in range(1, 5):
                @pl.when(n == size)
                def _():
                    pltpu.make_async_copy(
                        kv_ref.at[img // 4, 0:size, lax.rem(img, 4)], buf.at[r, pl.ds(pos, size)], kv_sem.at[r]
                    ).start()
            return pos + n

        return lax.fori_loop(0, 32, slot, 0)

    counts = [fetch(0), fetch(1)]
    writes = []
    for r in range(2):
        n = counts[r]
        clear(m_ref, l_ref, a_ref)
        if r == 0:
            for c in reads + carried[:4]:
                c.wait()
            for c in carried[4:]:
                c.start()

        def arrived(p, carry):
            ref = buf.at[r, 0]
            pltpu.make_async_copy(ref, ref, kv_sem.at[r]).wait()
            return carry

        lax.fori_loop(0, n, arrived, 0)

        def blank(p, carry):
            buf[r, p, 1] = jnp.zeros((TILE, 256), jnp.bfloat16)
            return carry

        lax.fori_loop(n, (n + 7) // 8 * 8, blank, 0)

        def chunk(c, size, masked):
            at = pl.ds(c * per, size // TILE)
            for j in range(2):
                cols = slice(j * 128, (j + 1) * 128)
                rows = slice(j * 1024, (j + 1) * 1024)
                sc = lax.dot_general(
                    qs[r * 2048 + j * 1024:r * 2048 + (j + 1) * 1024, :], buf[r, at, 0, :, cols].reshape(size, 128), NT,
                    preferred_element_type=jnp.float32,
                )
                if masked:
                    keys = lax.broadcasted_iota(jnp.int32, sc.shape, 1)
                    sc = jnp.where(keys < n * TILE - c * CHUNK, sc, NEG)
                softmax_step(sc, m_ref, l_ref, a_ref, buf[r, at, 1, :, cols].reshape(size, 128), rows)

        full = n // per
        left = n - full * per

        def body(c, carry):
            chunk(c, CHUNK, False)
            return carry

        lax.fori_loop(0, full, body, 0)

        @pl.when(left > per // 2)
        def _():
            chunk(full, CHUNK, True)

        @pl.when((left > 0) & (left <= per // 2))
        def _():
            chunk(full, CHUNK // 2, True)

        for i in range(16):
            rows = slice(i * 128, (i + 1) * 128)
            to = slice(r * 2048 + i * 128, r * 2048 + (i + 1) * 128)
            total = jnp.sum(l_ref[rows, :], axis=1, keepdims=True)
            os[to, :] = (a_ref[rows, :] / jnp.maximum(total, 1.0)).astype(jnp.bfloat16)
            c = pltpu.make_async_copy(os.at[to, :], out_ref.at[r * 128:(r + 1) * 128, i * 128:(i + 1) * 128], o_sem.at[r, i])
            c.start()
            writes.append(c)
    for c in writes + carried[4:]:
        c.wait()


def local(self_q, self_k, self_v, doc_ids, cross_q, image_keys, image_values, image_list, image_lengths, cross_mask):
    bf16, f32, i32 = jnp.bfloat16, jnp.float32, jnp.int32
    hbm = pl.BlockSpec(memory_space=pltpu.HBM)
    dma = lambda *shape: pltpu.SemaphoreType.DMA(shape)
    place = lambda x: pltpu.with_memory_space_constraint(x, pltpu.HBM)
    kv, attended = pl.pallas_call(
        exchange,
        name="exchange",
        out_shape=(pltpu.HBM((32, 4, 4, 2, TILE, 256), bf16), pltpu.HBM((256, 2048), bf16)),
        in_specs=[hbm] * 6,
        out_specs=(hbm, hbm),
        scratch_shapes=[
            pltpu.VMEM((4096, 128), bf16), pltpu.VMEM((4096, 128), bf16), pltpu.VMEM((4, 2, TILE, 256), bf16),
            pltpu.VMEM((1280, 256), bf16), pltpu.VMEM((1280, 256), bf16),
            pltpu.VMEM((1, 2048), i32), pltpu.VMEM((256, 1280), f32),
            pltpu.VMEM((4096, 128), f32), pltpu.VMEM((4096, 128), f32), pltpu.VMEM((4096, 128), f32),
            dma(3, 2), dma(3, 2), dma(1), dma(3, 5), dma(3, 5), dma(4, 3, 5), dma(4, 3, 5),
            dma(4, 4, 5), dma(4, 4, 5), dma(6, 2), dma(6, 2), dma(21), dma(16),
        ],
        compiler_params=pltpu.CompilerParams(collective_id=0, has_side_effects=True, vmem_limit_bytes=48 << 20),
    )(*(place(x) for x in (image_keys, image_values, self_k[0], self_v[0], doc_ids, self_q[0])))
    cross_out, self_out = pl.pallas_call(
        cross_kernel,
        name="cross_attend",
        out_shape=(pltpu.HBM((256, 2048), bf16), pltpu.HBM((256, 2048), bf16)),
        in_specs=[hbm] * 6,
        out_specs=(hbm, hbm),
        scratch_shapes=[
            pltpu.SMEM((4, 8, 32), i32), pltpu.SMEM((128,), i32), pltpu.SMEM((1, 2, 32), i32),
            pltpu.VMEM((4096, 128), bf16), pltpu.VMEM((4096, 128), bf16), pltpu.VMEM((2, 128, 2, TILE, 256), bf16), pltpu.VMEM((256, 2048), bf16),
            pltpu.VMEM((2048, 128), f32), pltpu.VMEM((2048, 128), f32), pltpu.VMEM((2048, 128), f32),
            dma(3), dma(2, 16), dma(2, 16), dma(2), dma(2, 4),
        ],
        compiler_params=pltpu.CompilerParams(vmem_limit_bytes=48 << 20),
    )(*(place(x) for x in (image_list, image_lengths, cross_mask, cross_q[0])), place(kv), place(attended))
    return self_out[None], cross_out[None]


def solution(mesh):
    in_specs = (
        P("enc", "seq", "mp"),
        P("enc", "seq", "mp"),
        P("enc", "seq", "mp"),
        P("enc", None),
        P("enc", "seq", "mp"),
        P(("seq", "enc"), "mp", None),
        P(("seq", "enc"), "mp", None),
        P(),
        P(),
        P("enc", "seq", None),
    )
    out_specs = (P("enc", "seq", "mp"), P("enc", "seq", "mp"))
    return jax.shard_map(local, mesh=mesh, in_specs=in_specs, out_specs=out_specs, check_vma=False)
```

```python
import functools
import jax
import jax.numpy as jnp
from jax import lax
from jax.experimental import pallas as pl
from jax.experimental.pallas import tpu as pltpu
from jax.sharding import PartitionSpec as P

HD = 128
NEG = -1e30
START = -5e29
LOG2E = 1.4426950408889634
FACTOR = HD ** (-0.5) * LOG2E
MESH = pl.DeviceIdType.MESH
TILE = 32
CHUNK = 512
NT = (((1,), (1,)), ((), ()))


def softmax_step(sc, m_ref, l_ref, a_ref, v, rows):
    n = sc.shape[1] // 128
    m_old = m_ref[rows, :]
    m_new = jnp.maximum(m_old, jnp.max(sc, axis=1, keepdims=True))
    p = jnp.exp2((sc - jnp.concatenate([m_new] * n, axis=1)) * FACTOR)
    alpha = jnp.exp2((m_old - m_new) * FACTOR)
    part = p[:, 0:128]
    for i in range(1, n):
        part = part + p[:, i * 128:(i + 1) * 128]
    l_ref[rows, :] = l_ref[rows, :] * alpha + part
    a_ref[rows, :] = a_ref[rows, :] * alpha + jnp.dot(p.astype(jnp.bfloat16), v, preferred_element_type=jnp.float32)
    m_ref[rows, :] = m_new


def clear(m_ref, l_ref, a_ref):
    m_ref[...] = jnp.full_like(m_ref, START)
    l_ref[...] = jnp.zeros_like(l_ref)
    a_ref[...] = jnp.zeros_like(a_ref)


def exchange(
    ik, iv, sk, sv, ids, sq, kv, self_out, qs, os, own, kbuf, vbuf, docs, bias, m_ref, l_ref, a_ref,
    mp_s, mp_r, own_s, r1_s, r1_r, r2_s, r2_r, sib_s, sib_r, tx_s, tx_r, load_sem, out_sem,
):
    s = lax.axis_index("seq")
    g = lax.axis_index("mp")
    e = lax.axis_index("enc")
    core = lax.rem(s, 2)
    y = s // 2
    sibling = (s + 1 - 2 * core, g, e)
    me = s * 4 + e

    def place(order):
        return e + order * (y - e), y + order * (e - y)

    steps = (lambda p: p, lambda p: lax.rem(p + 3, 4), lambda p: lax.rem(p + 1, 4), lambda p: lax.rem(p + 2, 4))

    def spot(i1, i2, order):
        p1, p2 = place(order)
        q1, q2 = steps[i1](p1), steps[i2](p2)
        return q2 + order * (q1 - q2), q1 + order * (q2 - q1)

    def at(i1, i2, order):
        yy, zz = spot(i1, i2, order)
        return (2 * yy + core, g, zz)

    def piece(i1, i2, order, of=core):
        yy, zz = spot(i1, i2, order)
        return (2 * yy + of) * 4 + zz

    turn = (g, lax.rem(g + 3, 4), lax.rem(g + 1, 4), lax.rem(g + 2, 4))
    chunks = (
        (turn[0], slice(0, 4), core), (turn[1], slice(0, 4), core), (turn[2], slice(0, 4), core),
        (turn[3], slice(0, 2), core), (turn[3], slice(2, 4), 1),
    )

    loads = [
        pltpu.make_async_copy(ids, docs, load_sem.at[0]),
        pltpu.make_async_copy(sk, kbuf.at[0:256, :], load_sem.at[1]),
        pltpu.make_async_copy(sv, vbuf.at[0:256, :], load_sem.at[2]),
    ]
    own_cols = pl.ds(pl.multiple_of(g * 256, 256), 256)
    bring = [
        pltpu.make_async_copy(src.at[:, :, own_cols], own.at[:, half], load_sem.at[19 + half]) for half, src in ((0, ik), (1, iv))
    ]
    for i in range(16):
        loads.append(pltpu.make_async_copy(sq.at[:, i * 128:(i + 1) * 128], qs.at[i * 256:(i + 1) * 256, :], load_sem.at[3 + i]))

    barrier = pltpu.get_barrier_semaphore()
    greet = [at(2, 0, core), at(1, 0, core), at(0, 2, core), at(0, 1, core), sibling] + [(s, lax.rem(g + d, 4), e) for d in (1, 2, 3)]
    for who in greet:
        pl.semaphore_signal(barrier, inc=1, device_id=who, device_id_type=MESH)
    for c in bring + loads:
        c.start()
    pl.semaphore_wait(barrier, len(greet))

    def remote(src, dst, ss, rs, who):
        return pltpu.make_async_remote_copy(
            src_ref=src, dst_ref=dst, send_sem=ss, recv_sem=rs, device_id=who, device_id_type=MESH
        )

    sends = []

    def go(src, dst, ss, rs, who, cond=None):
        r = remote(src, dst, ss, rs, who)
        sends.append((cond, r))
        if cond is None:
            r.start()
        else:
            @pl.when(cond)
            def _():
                r.start()

    def block(h, c):
        return kv.at[h, chunks[c][0], chunks[c][1]]

    def landed(h, c, rs):
        pltpu.make_async_copy(block(h, c), block(h, c), rs).wait()

    arriving = {}
    for d in (1, 3, 2):
        to = lax.rem(g + d, 4)
        cols = pl.ds(pl.multiple_of(to * 256, 256), 256)
        for half, src in ((0, ik), (1, iv)):
            r = remote(src.at[:, :, cols], kv.at[me, g, :, half], mp_s.at[d - 1, half], mp_r.at[d - 1, half], (s, to, e))
            r.start()
            arriving[d, half] = r

    text = []

    def guarded(cond, r):
        text.append((cond, r))

        @pl.when(cond)
        def _():
            r.start()

    def text_at(buf, d):
        return buf.at[256 * d:256 * (d + 1), :]

    def text_landed(cond, d, half, sem):
        @pl.when(cond)
        def _():
            ref = text_at((kbuf, vbuf)[half], d)
            pltpu.make_async_copy(ref, ref, sem).wait()

    ahead = (lax.rem(s + 2, 8), g, e)
    for half, src in ((0, sk), (1, sv)):
        buf = (kbuf, vbuf)[half]
        guarded(s + 2 < 8, remote(src, text_at(buf, 2), tx_s.at[0, half], tx_r.at[0, half], ahead))
        guarded(core == 0, remote(src, text_at(buf, 1), tx_s.at[1, half], tx_r.at[1, half], sibling))
    for d in range(1, 5):
        @pl.when(s < d)
        def _():
            for buf in (kbuf, vbuf):
                buf[256 * d:256 * (d + 1), :] = jnp.zeros((256, 256), jnp.bfloat16)

    def text_onward():
        for half in (0, 1):
            buf = (kbuf, vbuf)[half]
            text_landed(s >= 2, 2, half, tx_r.at[0, half])
            got = text_at(buf, 2)
            guarded((s >= 2) & (s + 2 < 8), remote(got, text_at(buf, 4), tx_s.at[4, half], tx_r.at[4, half], ahead))
            guarded((s >= 2) & (core == 0), remote(got, text_at(buf, 3), tx_s.at[2, half], tx_r.at[2, half], sibling))
            guarded((s >= 2) & (core == 1), remote(got, text_at(buf, 1), tx_s.at[3, half], tx_r.at[3, half], sibling))

    def text_near():
        for half in (0, 1):
            text_landed(core == 1, 1, half, tx_r.at[1, half])
            text_landed((s >= 2) & (core == 0), 1, half, tx_r.at[3, half])

    def text_far():
        for half in (0, 1):
            buf = (kbuf, vbuf)[half]
            text_landed(s >= 4, 4, half, tx_r.at[4, half])
            guarded((s >= 4) & (core == 1), remote(text_at(buf, 4), text_at(buf, 3), tx_s.at[5, half], tx_r.at[5, half], sibling))
        for half in (0, 1):
            text_landed((s >= 2) & (core == 1), 3, half, tx_r.at[2, half])
            text_landed((s >= 4) & (core == 0), 3, half, tx_r.at[5, half])

    def to_sibling(i1, i2, c, src=None):
        ref = block(piece(i1, i2, chunks[c][2]), c)
        go(ref if src is None else src, ref, sib_s.at[i1, i2, c], sib_r.at[i1, i2, c], sibling)

    def ring1(c, src=None):
        order = chunks[c][2]
        ref = block(me, c)
        go(ref if src is None else src, ref, r1_s.at[0, c], r1_r.at[0, c], at(2, 0, order))
        go(ref if src is None else src, ref, r1_s.at[1, c], r1_r.at[1, c], at(1, 0, order))

    def ring2(i1, c, src=None):
        order = chunks[c][2]
        ref = block(piece(i1, 0, order), c)
        go(ref if src is None else src, ref, r2_s.at[i1, 0, c], r2_r.at[i1, 0, c], at(0, 2, order))
        go(ref if src is None else src, ref, r2_s.at[i1, 1, c], r2_r.at[i1, 1, c], at(0, 1, order))

    def release(c, src=None):
        ring1(c, src)
        ring2(0, c, src)
        to_sibling(0, 0, c, src)

    def onward1(c):
        order = chunks[c][2]
        for i1, far, to in ((1, c < 2, at(2, 0, order)), (2, c >= 2, at(1, 0, order))):
            h = piece(i1, 0, order)
            landed(h, c, r1_r.at[i1 - 1, c])
            if far:
                go(block(h, c), block(h, c), r1_s.at[2, c], r1_r.at[2, c], to)
            ring2(i1, c)
            to_sibling(i1, 0, c)

    def onward2(i1, c):
        order = chunks[c][2]
        far = {0: (True, False), 1: (core == 1, core == 0)}.get(c, (False, True))
        for i2, cond, to in ((1, far[0], at(0, 2, order)), (2, far[1], at(0, 1, order))):
            h = piece(i1, i2, order)
            landed(h, c, r2_r.at[i1, i2 - 1, c])
            if cond is not False:
                go(block(h, c), block(h, c), r2_s.at[i1, 2, c], r2_r.at[i1, 2, c], to, None if cond is True else cond)
            to_sibling(i1, i2, c)

    def across1(c):
        landed(piece(3, 0, chunks[c][2]), c, r1_r.at[2, c])
        ring2(3, c)
        to_sibling(3, 0, c)

    def across2(i1, c):
        landed(piece(i1, 3, chunks[c][2]), c, r2_r.at[i1, 2, c])
        to_sibling(i1, 3, c)

    def self_setup():
        for c in loads:
            c.wait()

        def row_docs(block):
            return docs[:, pl.ds(pl.multiple_of(block * 256, 256), 256)].astype(jnp.float32)

        own = row_docs(s)
        column = jnp.concatenate(
            [jnp.transpose(jnp.broadcast_to(own[:, i * 128:(i + 1) * 128], (128, 128))) for i in (0, 1)], axis=0
        )
        column = jnp.concatenate([column, column], axis=1)
        rows = lax.broadcasted_iota(jnp.int32, (256, 256), 0)
        cols = lax.broadcasted_iota(jnp.int32, (256, 256), 1)
        bias[:, 0:256] = jnp.where((column == own) & (cols <= rows), 0.0, NEG)
        for d in range(1, 5):
            seen = (column == row_docs(jnp.maximum(s - d, 0))) & (rows - rows + s >= d)
            bias[:, d * 256:(d + 1) * 256] = jnp.where(seen, 0.0, NEG)

    def self_units(lo, hi, key, size):
        def unit(q, carry):
            cols = pl.ds(pl.multiple_of(q // 2 * 128, 128), 128)
            rows = pl.ds(pl.multiple_of(q * 1024, 1024), 1024)
            sc = lax.dot_general(qs[rows, :], kbuf[key:key + size, cols], NT, preferred_element_type=jnp.float32)
            sc = sc + jnp.concatenate([bias[:, key:key + size]] * 4, axis=0)
            softmax_step(sc, m_ref, l_ref, a_ref, vbuf[key:key + size, cols], rows)
            return carry

        lax.fori_loop(lo, hi, unit, 0)

    writes = []

    def emit():
        for i in range(16):
            rows = slice(i * 256, (i + 1) * 256)
            total = jnp.sum(l_ref[rows, :], axis=1, keepdims=True)
            os[rows, :] = (a_ref[rows, :] / jnp.maximum(total, 1.0)).astype(jnp.bfloat16)
            c = pltpu.make_async_copy(os.at[rows, :], self_out.at[:, i * 128:(i + 1) * 128], out_sem.at[i])
            c.start()
            writes.append(c)

    for r in bring:
        r.wait()
    keep = pltpu.make_async_copy(own, kv.at[me, g], own_s.at[0])
    keep.start()
    release(0, own)
    self_setup()
    clear(m_ref, l_ref, a_ref)
    for c, d in ((1, 1), (2, 3), (3, 2)):
        for half in (0, 1):
            arriving[d, half].wait_recv()
        release(c)
    release(4)
    text_onward()
    onward1(0)
    onward2(0, 0)
    text_near()
    self_units(0, 1, 0, 512)
    onward1(1)
    onward2(0, 1)
    self_units(1, 2, 0, 512)
    onward1(2)
    onward2(0, 2)
    self_units(2, 3, 0, 512)
    onward1(3)
    onward2(0, 3)
    onward1(4)
    onward2(0, 4)
    self_units(3, 4, 0, 512)
    text_far()
    for c in range(5):
        across1(c)
        for i1 in (1, 2):
            onward2(i1, c)
        if c < 4:
            self_units(c, c + 1, 512, 512)
    for c in range(5):
        onward2(3, c)
        if c < 4:
            self_units(c, c + 1, 1024, 256)
    emit()
    for i1 in range(4):
        for c in range(5):
            across2(i1, c)

    for i1 in range(4):
        for i2 in range(4):
            for c in range(5):
                order = 1 - core if c < 4 else 1
                landed(piece(i1, i2, order, 1 - core), c, sib_r.at[i1, i2, c])
    for cond, r in sends + text:
        if cond is None:
            r.wait_send()
        else:
            @pl.when(cond)
            def _():
                r.wait_send()
    keep.wait()
    for r in arriving.values():
        r.wait_send()
    for c in writes:
        c.wait()


def cross_kernel(lists, lengths, flags, q_ref, kv_ref, done, out_ref, self_ref, list_ref, len_ref, mask_ref, qs, os, buf, through, m_ref, l_ref, a_ref, t_sem, q_sem, o_sem, kv_sem, d_sem):
    s = lax.axis_index("seq")
    e = lax.axis_index("enc")
    per = CHUNK // TILE
    tables = [
        pltpu.make_async_copy(lists, list_ref, t_sem.at[0]),
        pltpu.make_async_copy(lengths, len_ref, t_sem.at[1]),
        pltpu.make_async_copy(flags, mask_ref, t_sem.at[2]),
    ]
    reads = [
        pltpu.make_async_copy(
            q_ref.at[r * 128:(r + 1) * 128, i * 128:(i + 1) * 128],
            qs.at[r * 2048 + i * 128:r * 2048 + (i + 1) * 128, :], q_sem.at[r, i],
        )
        for r in range(2) for i in range(16)
    ]
    carried = [
        pltpu.make_async_copy(a.at[i * 64:(i + 1) * 64, :], b.at[i * 64:(i + 1) * 64, :], d_sem.at[way, i])
        for way, (a, b) in enumerate(((done, through), (through, self_ref))) for i in range(4)
    ]
    for c in tables + reads + carried[:4]:
        c.start()
    clear(m_ref, l_ref, a_ref)
    for c in tables:
        c.wait()

    def fetch(r):
        def slot(k, pos):
            img = list_ref[e, s, k]
            n = jnp.where(mask_ref[0, r, k] == 1, len_ref[img] // TILE, 0)
            for size in range(1, 5):
                @pl.when(n == size)
                def _():
                    pltpu.make_async_copy(
                        kv_ref.at[img // 4, 0:size, lax.rem(img, 4)], buf.at[r, pl.ds(pos, size)], kv_sem.at[r]
                    ).start()
            return pos + n

        return lax.fori_loop(0, 32, slot, 0)

    counts = [fetch(0), fetch(1)]
    writes = []
    for r in range(2):
        n = counts[r]
        if r == 1:
            clear(m_ref, l_ref, a_ref)
        if r == 0:
            for c in reads + carried[:4]:
                c.wait()
            for c in carried[4:]:
                c.start()

        def arrived(p, carry):
            ref = buf.at[r, 0]
            pltpu.make_async_copy(ref, ref, kv_sem.at[r]).wait()
            return carry

        lax.fori_loop(0, n, arrived, 0)

        def blank(p, carry):
            buf[r, p, 1] = jnp.zeros((TILE, 256), jnp.bfloat16)
            return carry

        lax.fori_loop(n, (n + 7) // 8 * 8, blank, 0)

        def chunk(c, size, masked):
            at = pl.ds(c * per, size // TILE)
            heads = [(slice(j * 128, (j + 1) * 128), slice(j * 1024, (j + 1) * 1024)) for j in range(2)]
            scores = [
                lax.dot_general(
                    qs[r * 2048 + rows.start:r * 2048 + rows.stop, :], buf[r, at, 0, :, cols].reshape(size, 128), NT,
                    preferred_element_type=jnp.float32,
                )
                for cols, rows in heads
            ]
            if masked:
                live = lax.broadcasted_iota(jnp.int32, scores[0].shape, 1) < n * TILE - c * CHUNK
                scores = [jnp.where(live, sc, NEG) for sc in scores]
            for sc, (cols, rows) in zip(scores, heads):
                softmax_step(sc, m_ref, l_ref, a_ref, buf[r, at, 1, :, cols].reshape(size, 128), rows)

        full = n // per
        left = n - full * per

        def body(c, carry):
            chunk(c, CHUNK, False)
            return carry

        lax.fori_loop(0, full, body, 0)

        @pl.when(left > per // 2)
        def _():
            chunk(full, CHUNK, True)

        @pl.when((left > 0) & (left <= per // 2))
        def _():
            chunk(full, CHUNK // 2, True)

        for i in range(16):
            rows = slice(i * 128, (i + 1) * 128)
            to = slice(r * 2048 + i * 128, r * 2048 + (i + 1) * 128)
            total = jnp.sum(l_ref[rows, :], axis=1, keepdims=True)
            os[to, :] = (a_ref[rows, :] * (1.0 / jnp.maximum(total, 1.0))).astype(jnp.bfloat16)
            c = pltpu.make_async_copy(os.at[to, :], out_ref.at[r * 128:(r + 1) * 128, i * 128:(i + 1) * 128], o_sem.at[r, i])
            c.start()
            writes.append(c)
    for c in writes + carried[4:]:
        c.wait()


def local(self_q, self_k, self_v, doc_ids, cross_q, image_keys, image_values, image_list, image_lengths, cross_mask):
    bf16, f32, i32 = jnp.bfloat16, jnp.float32, jnp.int32
    hbm = pl.BlockSpec(memory_space=pltpu.HBM)
    dma = lambda *shape: pltpu.SemaphoreType.DMA(shape)
    place = lambda x: pltpu.with_memory_space_constraint(x, pltpu.HBM)
    kv, attended = pl.pallas_call(
        exchange,
        name="exchange",
        out_shape=(pltpu.HBM((32, 4, 4, 2, TILE, 256), bf16), pltpu.HBM((256, 2048), bf16)),
        in_specs=[hbm] * 6,
        out_specs=(hbm, hbm),
        scratch_shapes=[
            pltpu.VMEM((4096, 128), bf16), pltpu.VMEM((4096, 128), bf16), pltpu.VMEM((4, 2, TILE, 256), bf16),
            pltpu.VMEM((1280, 256), bf16), pltpu.VMEM((1280, 256), bf16),
            pltpu.VMEM((1, 2048), i32), pltpu.VMEM((256, 1280), f32),
            pltpu.VMEM((4096, 128), f32), pltpu.VMEM((4096, 128), f32), pltpu.VMEM((4096, 128), f32),
            dma(3, 2), dma(3, 2), dma(1), dma(3, 5), dma(3, 5), dma(4, 3, 5), dma(4, 3, 5),
            dma(4, 4, 5), dma(4, 4, 5), dma(6, 2), dma(6, 2), dma(21), dma(16),
        ],
        compiler_params=pltpu.CompilerParams(collective_id=0, has_side_effects=True, vmem_limit_bytes=48 << 20),
    )(*(place(x) for x in (image_keys, image_values, self_k[0], self_v[0], doc_ids, self_q[0])))
    cross_out, self_out = pl.pallas_call(
        cross_kernel,
        name="cross_attend",
        out_shape=(pltpu.HBM((256, 2048), bf16), pltpu.HBM((256, 2048), bf16)),
        in_specs=[hbm] * 6,
        out_specs=(hbm, hbm),
        scratch_shapes=[
            pltpu.SMEM((4, 8, 32), i32), pltpu.SMEM((128,), i32), pltpu.SMEM((1, 2, 32), i32),
            pltpu.VMEM((4096, 128), bf16), pltpu.VMEM((4096, 128), bf16), pltpu.VMEM((2, 128, 2, TILE, 256), bf16), pltpu.VMEM((256, 2048), bf16),
            pltpu.VMEM((2048, 128), f32), pltpu.VMEM((2048, 128), f32), pltpu.VMEM((2048, 128), f32),
            dma(3), dma(2, 16), dma(2, 16), dma(2), dma(2, 4),
        ],
        compiler_params=pltpu.CompilerParams(vmem_limit_bytes=48 << 20),
    )(*(place(x) for x in (image_list, image_lengths, cross_mask, cross_q[0])), place(kv), place(attended))
    return self_out[None], cross_out[None]


def solution(mesh):
    in_specs = (
        P("enc", "seq", "mp"),
        P("enc", "seq", "mp"),
        P("enc", "seq", "mp"),
        P("enc", None),
        P("enc", "seq", "mp"),
        P(("seq", "enc"), "mp", None),
        P(("seq", "enc"), "mp", None),
        P(),
        P(),
        P("enc", "seq", None),
    )
    out_specs = (P("enc", "seq", "mp"), P("enc", "seq", "mp"))
    return jax.shard_map(local, mesh=mesh, in_specs=in_specs, out_specs=out_specs, check_vma=False)
```

```python
import functools
import jax
import jax.numpy as jnp
from jax import lax
from jax.experimental import pallas as pl
from jax.experimental.pallas import tpu as pltpu
from jax.sharding import PartitionSpec as P

HD = 128
NEG = -1e30
START = -5e29
LOG2E = 1.4426950408889634
FACTOR = HD ** (-0.5) * LOG2E
MESH = pl.DeviceIdType.MESH
TILE = 32
CHUNK = 512
NT = (((1,), (1,)), ((), ()))


def softmax_step(sc, m_ref, l_ref, a_ref, v, rows):
    n = sc.shape[1] // 128
    m_old = m_ref[rows, :]
    m_new = jnp.maximum(m_old, jnp.max(sc, axis=1, keepdims=True))
    p = jnp.exp2((sc - jnp.concatenate([m_new] * n, axis=1)) * FACTOR)
    alpha = jnp.exp2((m_old - m_new) * FACTOR)
    part = p[:, 0:128]
    for i in range(1, n):
        part = part + p[:, i * 128:(i + 1) * 128]
    l_ref[rows, :] = l_ref[rows, :] * alpha + part
    a_ref[rows, :] = a_ref[rows, :] * alpha + jnp.dot(p.astype(jnp.bfloat16), v, preferred_element_type=jnp.float32)
    m_ref[rows, :] = m_new


def clear(m_ref, l_ref, a_ref):
    m_ref[...] = jnp.full_like(m_ref, START)
    l_ref[...] = jnp.zeros_like(l_ref)
    a_ref[...] = jnp.zeros_like(a_ref)


def exchange(
    ik, iv, sk, sv, ids, sq, kv, self_out, qs, os, own, kbuf, vbuf, docs, bias, m_ref, l_ref, a_ref,
    mp_s, mp_r, own_s, r1_s, r1_r, r2_s, r2_r, sib_s, sib_r, tx_s, tx_r, load_sem, out_sem,
):
    s = lax.axis_index("seq")
    g = lax.axis_index("mp")
    e = lax.axis_index("enc")
    core = lax.rem(s, 2)
    y = s // 2
    sibling = (s + 1 - 2 * core, g, e)
    me = s * 4 + e

    def place(order):
        return e + order * (y - e), y + order * (e - y)

    steps = (lambda p: p, lambda p: lax.rem(p + 3, 4), lambda p: lax.rem(p + 1, 4), lambda p: lax.rem(p + 2, 4))

    def spot(i1, i2, order):
        p1, p2 = place(order)
        q1, q2 = steps[i1](p1), steps[i2](p2)
        return q2 + order * (q1 - q2), q1 + order * (q2 - q1)

    def at(i1, i2, order):
        yy, zz = spot(i1, i2, order)
        return (2 * yy + core, g, zz)

    def piece(i1, i2, order, of=core):
        yy, zz = spot(i1, i2, order)
        return (2 * yy + of) * 4 + zz

    turn = (g, lax.rem(g + 3, 4), lax.rem(g + 1, 4), lax.rem(g + 2, 4))
    chunks = (
        (turn[0], slice(0, 4), core), (turn[1], slice(0, 4), core), (turn[2], slice(0, 4), core),
        (turn[3], slice(0, 2), core), (turn[3], slice(2, 4), 1),
    )

    loads = [
        pltpu.make_async_copy(ids, docs, load_sem.at[0]),
        pltpu.make_async_copy(sk, kbuf.at[0:256, :], load_sem.at[1]),
        pltpu.make_async_copy(sv, vbuf.at[0:256, :], load_sem.at[2]),
    ]
    own_cols = pl.ds(pl.multiple_of(g * 256, 256), 256)
    bring = [
        pltpu.make_async_copy(src.at[:, :, own_cols], own.at[:, half], load_sem.at[19 + half]) for half, src in ((0, ik), (1, iv))
    ]
    for i in range(16):
        loads.append(pltpu.make_async_copy(sq.at[:, i * 128:(i + 1) * 128], qs.at[i * 256:(i + 1) * 256, :], load_sem.at[3 + i]))

    barrier = pltpu.get_barrier_semaphore()
    greet = [at(2, 0, core), at(1, 0, core), at(0, 2, core), at(0, 1, core), sibling] + [(s, lax.rem(g + d, 4), e) for d in (1, 2, 3)]
    for who in greet:
        pl.semaphore_signal(barrier, inc=1, device_id=who, device_id_type=MESH)
    for c in bring + loads:
        c.start()
    pl.semaphore_wait(barrier, len(greet))

    def remote(src, dst, ss, rs, who):
        return pltpu.make_async_remote_copy(
            src_ref=src, dst_ref=dst, send_sem=ss, recv_sem=rs, device_id=who, device_id_type=MESH
        )

    sends = []

    def go(src, dst, ss, rs, who, cond=None):
        r = remote(src, dst, ss, rs, who)
        sends.append((cond, r))
        if cond is None:
            r.start()
        else:
            @pl.when(cond)
            def _():
                r.start()

    def block(h, c):
        return kv.at[h, chunks[c][0], chunks[c][1]]

    def landed(h, c, rs):
        pltpu.make_async_copy(block(h, c), block(h, c), rs).wait()

    arriving = {}
    for d in (1, 3, 2):
        to = lax.rem(g + d, 4)
        cols = pl.ds(pl.multiple_of(to * 256, 256), 256)
        for half, src in ((0, ik), (1, iv)):
            r = remote(src.at[:, :, cols], kv.at[me, g, :, half], mp_s.at[d - 1, half], mp_r.at[d - 1, half], (s, to, e))
            r.start()
            arriving[d, half] = r

    text = []

    def guarded(cond, r):
        text.append((cond, r))

        @pl.when(cond)
        def _():
            r.start()

    def text_at(buf, d):
        return buf.at[256 * d:256 * (d + 1), :]

    def text_landed(cond, d, half, sem):
        @pl.when(cond)
        def _():
            ref = text_at((kbuf, vbuf)[half], d)
            pltpu.make_async_copy(ref, ref, sem).wait()

    ahead = (lax.rem(s + 2, 8), g, e)
    for half, src in ((0, sk), (1, sv)):
        buf = (kbuf, vbuf)[half]
        guarded(s + 2 < 8, remote(src, text_at(buf, 2), tx_s.at[0, half], tx_r.at[0, half], ahead))
        guarded(core == 0, remote(src, text_at(buf, 1), tx_s.at[1, half], tx_r.at[1, half], sibling))
    for d in range(1, 5):
        @pl.when(s < d)
        def _():
            for buf in (kbuf, vbuf):
                buf[256 * d:256 * (d + 1), :] = jnp.zeros((256, 256), jnp.bfloat16)

    def text_onward():
        for half in (0, 1):
            buf = (kbuf, vbuf)[half]
            text_landed(s >= 2, 2, half, tx_r.at[0, half])
            got = text_at(buf, 2)
            guarded((s >= 2) & (s + 2 < 8), remote(got, text_at(buf, 4), tx_s.at[4, half], tx_r.at[4, half], ahead))
            guarded((s >= 2) & (core == 0), remote(got, text_at(buf, 3), tx_s.at[2, half], tx_r.at[2, half], sibling))
            guarded((s >= 2) & (core == 1), remote(got, text_at(buf, 1), tx_s.at[3, half], tx_r.at[3, half], sibling))

    def text_near():
        for half in (0, 1):
            text_landed(core == 1, 1, half, tx_r.at[1, half])
            text_landed((s >= 2) & (core == 0), 1, half, tx_r.at[3, half])

    def text_far():
        for half in (0, 1):
            buf = (kbuf, vbuf)[half]
            text_landed(s >= 4, 4, half, tx_r.at[4, half])
            guarded((s >= 4) & (core == 1), remote(text_at(buf, 4), text_at(buf, 3), tx_s.at[5, half], tx_r.at[5, half], sibling))
        for half in (0, 1):
            text_landed((s >= 2) & (core == 1), 3, half, tx_r.at[2, half])
            text_landed((s >= 4) & (core == 0), 3, half, tx_r.at[5, half])

    def to_sibling(i1, i2, c, src=None):
        ref = block(piece(i1, i2, chunks[c][2]), c)
        go(ref if src is None else src, ref, sib_s.at[i1, i2, c], sib_r.at[i1, i2, c], sibling)

    def ring1(c, src=None):
        order = chunks[c][2]
        ref = block(me, c)
        go(ref if src is None else src, ref, r1_s.at[0, c], r1_r.at[0, c], at(2, 0, order))
        go(ref if src is None else src, ref, r1_s.at[1, c], r1_r.at[1, c], at(1, 0, order))

    def ring2(i1, c, src=None):
        order = chunks[c][2]
        ref = block(piece(i1, 0, order), c)
        go(ref if src is None else src, ref, r2_s.at[i1, 0, c], r2_r.at[i1, 0, c], at(0, 2, order))
        go(ref if src is None else src, ref, r2_s.at[i1, 1, c], r2_r.at[i1, 1, c], at(0, 1, order))

    def release(c, src=None):
        ring1(c, src)
        ring2(0, c, src)
        to_sibling(0, 0, c, src)

    def onward1(c):
        order = chunks[c][2]
        for i1, far, to in ((1, c < 2, at(2, 0, order)), (2, c >= 2, at(1, 0, order))):
            h = piece(i1, 0, order)
            landed(h, c, r1_r.at[i1 - 1, c])
            if far:
                go(block(h, c), block(h, c), r1_s.at[2, c], r1_r.at[2, c], to)
            ring2(i1, c)
            to_sibling(i1, 0, c)

    def onward2(i1, c):
        order = chunks[c][2]
        far = {0: (True, False), 1: (core == 1, core == 0)}.get(c, (False, True))
        for i2, cond, to in ((1, far[0], at(0, 2, order)), (2, far[1], at(0, 1, order))):
            h = piece(i1, i2, order)
            landed(h, c, r2_r.at[i1, i2 - 1, c])
            if cond is not False:
                go(block(h, c), block(h, c), r2_s.at[i1, 2, c], r2_r.at[i1, 2, c], to, None if cond is True else cond)
            to_sibling(i1, i2, c)

    def across1(c):
        landed(piece(3, 0, chunks[c][2]), c, r1_r.at[2, c])
        ring2(3, c)
        to_sibling(3, 0, c)

    def across2(i1, c):
        landed(piece(i1, 3, chunks[c][2]), c, r2_r.at[i1, 2, c])
        to_sibling(i1, 3, c)

    def self_setup():
        for c in loads:
            c.wait()

        def row_docs(block):
            return docs[:, pl.ds(pl.multiple_of(block * 256, 256), 256)].astype(jnp.float32)

        own = row_docs(s)
        column = jnp.concatenate(
            [jnp.transpose(jnp.broadcast_to(own[:, i * 128:(i + 1) * 128], (128, 128))) for i in (0, 1)], axis=0
        )
        column = jnp.concatenate([column, column], axis=1)
        rows = lax.broadcasted_iota(jnp.int32, (256, 256), 0)
        cols = lax.broadcasted_iota(jnp.int32, (256, 256), 1)
        bias[:, 0:256] = jnp.where((column == own) & (cols <= rows), 0.0, NEG)
        for d in range(1, 5):
            seen = (column == row_docs(jnp.maximum(s - d, 0))) & (rows - rows + s >= d)
            bias[:, d * 256:(d + 1) * 256] = jnp.where(seen, 0.0, NEG)

    def self_units(lo, hi, key, size):
        def unit(q, carry):
            cols = pl.ds(pl.multiple_of(q // 2 * 128, 128), 128)
            rows = pl.ds(pl.multiple_of(q * 1024, 1024), 1024)
            sc = lax.dot_general(qs[rows, :], kbuf[key:key + size, cols], NT, preferred_element_type=jnp.float32)
            sc = sc + jnp.concatenate([bias[:, key:key + size]] * 4, axis=0)
            softmax_step(sc, m_ref, l_ref, a_ref, vbuf[key:key + size, cols], rows)
            return carry

        lax.fori_loop(lo, hi, unit, 0)

    writes = []

    def emit():
        for i in range(16):
            rows = slice(i * 256, (i + 1) * 256)
            total = jnp.sum(l_ref[rows, :], axis=1, keepdims=True)
            os[rows, :] = (a_ref[rows, :] / jnp.maximum(total, 1.0)).astype(jnp.bfloat16)
            c = pltpu.make_async_copy(os.at[rows, :], self_out.at[:, i * 128:(i + 1) * 128], out_sem.at[i])
            c.start()
            writes.append(c)

    for r in bring:
        r.wait()
    keep = pltpu.make_async_copy(own, kv.at[me, g], own_s.at[0])
    keep.start()
    release(0, own)
    self_setup()
    clear(m_ref, l_ref, a_ref)
    for c, d in ((1, 1), (2, 3), (3, 2)):
        for half in (0, 1):
            arriving[d, half].wait_recv()
        release(c)
    release(4)
    text_onward()
    onward1(0)
    onward2(0, 0)
    text_near()
    self_units(0, 1, 0, 512)
    onward1(1)
    onward2(0, 1)
    self_units(1, 2, 0, 512)
    onward1(2)
    onward2(0, 2)
    self_units(2, 3, 0, 512)
    onward1(3)
    onward2(0, 3)
    onward1(4)
    onward2(0, 4)
    self_units(3, 4, 0, 512)
    text_far()
    for c in range(5):
        across1(c)
        for i1 in (1, 2):
            onward2(i1, c)
        if c < 4:
            self_units(c, c + 1, 512, 512)
    for c in range(5):
        onward2(3, c)
        if c < 4:
            self_units(c, c + 1, 1024, 256)
    emit()
    for i1 in range(4):
        for c in range(5):
            across2(i1, c)

    for i1 in range(4):
        for i2 in range(4):
            for c in range(5):
                order = 1 - core if c < 4 else 1
                landed(piece(i1, i2, order, 1 - core), c, sib_r.at[i1, i2, c])
    for cond, r in sends + text:
        if cond is None:
            r.wait_send()
        else:
            @pl.when(cond)
            def _():
                r.wait_send()
    keep.wait()
    for r in arriving.values():
        r.wait_send()
    for c in writes:
        c.wait()


def cross_kernel(lists, lengths, flags, q_ref, kv_ref, done, out_ref, self_ref, list_ref, len_ref, mask_ref, qs, os, buf, through, m_ref, l_ref, a_ref, t_sem, q_sem, o_sem, kv_sem, d_sem):
    s = lax.axis_index("seq")
    e = lax.axis_index("enc")
    per = CHUNK // TILE
    tables = [
        pltpu.make_async_copy(lists, list_ref, t_sem.at[0]),
        pltpu.make_async_copy(lengths, len_ref, t_sem.at[1]),
        pltpu.make_async_copy(flags, mask_ref, t_sem.at[2]),
    ]
    reads = [
        pltpu.make_async_copy(
            q_ref.at[r * 128:(r + 1) * 128, i * 128:(i + 1) * 128],
            qs.at[r * 2048 + i * 128:r * 2048 + (i + 1) * 128, :], q_sem.at[r, i],
        )
        for r in range(2) for i in range(16)
    ]
    carried = [
        pltpu.make_async_copy(a.at[i * 64:(i + 1) * 64, :], b.at[i * 64:(i + 1) * 64, :], d_sem.at[way, i])
        for way, (a, b) in enumerate(((done, through), (through, self_ref))) for i in range(4)
    ]
    for c in tables + reads + carried[:4]:
        c.start()
    clear(m_ref, l_ref, a_ref)
    for c in tables:
        c.wait()

    def fetch(r):
        def slot(k, pos):
            img = list_ref[e, s, k]
            n = jnp.where(mask_ref[0, r, k] == 1, len_ref[img] // TILE, 0)
            for size in range(1, 5):
                @pl.when(n == size)
                def _():
                    pltpu.make_async_copy(
                        kv_ref.at[img // 4, 0:size, lax.rem(img, 4)], buf.at[r, pl.ds(pos, size)], kv_sem.at[r]
                    ).start()
            return pos + n

        return lax.fori_loop(0, 32, slot, 0)

    counts = [fetch(0), fetch(1)]
    writes = []
    for r in range(2):
        n = counts[r]
        for copy in reads[16 * r:16 * (r + 1)]:
            copy.wait()

        def arrived(p, carry):
            ref = buf.at[r, 0]
            pltpu.make_async_copy(ref, ref, kv_sem.at[r]).wait()
            return carry

        lax.fori_loop(0, n, arrived, 0)

        def blank(p, carry):
            buf[r, p, 1] = jnp.zeros((TILE, 256), jnp.bfloat16)
            return carry

        lax.fori_loop(n, (n + 7) // 8 * 8, blank, 0)

        def chunk(c, size, masked):
            at = pl.ds(c * per, size // TILE)
            heads = [(slice(j * 128, (j + 1) * 128), slice(r * 2048 + j * 1024, r * 2048 + (j + 1) * 1024)) for j in range(2)]
            scores = [
                lax.dot_general(
                    qs[rows, :], buf[r, at, 0, :, cols].reshape(size, 128), NT,
                    preferred_element_type=jnp.float32,
                )
                for cols, rows in heads
            ]
            if masked:
                live = lax.broadcasted_iota(jnp.int32, scores[0].shape, 1) < n * TILE - c * CHUNK
                scores = [jnp.where(live, sc, NEG) for sc in scores]
            for sc, (cols, rows) in zip(scores, heads):
                softmax_step(sc, m_ref, l_ref, a_ref, buf[r, at, 1, :, cols].reshape(size, 128), rows)

        full = n // per
        left = n - full * per

        def body(c, carry):
            chunk(c, CHUNK, False)
            return carry

        lax.fori_loop(0, full, body, 0)

        @pl.when(left > per // 2)
        def _():
            chunk(full, CHUNK, True)

        @pl.when((left > 0) & (left <= per // 2))
        def _():
            chunk(full, CHUNK // 2, True)

        if r == 0:
            for copy in carried[:4]:
                copy.wait()
            for copy in carried[4:]:
                copy.start()
        for i in range(16):
            rows = to = slice(r * 2048 + i * 128, r * 2048 + (i + 1) * 128)
            total = jnp.sum(l_ref[rows, :], axis=1, keepdims=True)
            os[to, :] = (a_ref[rows, :] * (1.0 / jnp.maximum(total, 1.0))).astype(jnp.bfloat16)
            c = pltpu.make_async_copy(os.at[to, :], out_ref.at[r * 128:(r + 1) * 128, i * 128:(i + 1) * 128], o_sem.at[r, i])
            c.start()
            writes.append(c)
    for c in writes + carried[4:]:
        c.wait()


def local(self_q, self_k, self_v, doc_ids, cross_q, image_keys, image_values, image_list, image_lengths, cross_mask):
    bf16, f32, i32 = jnp.bfloat16, jnp.float32, jnp.int32
    hbm = pl.BlockSpec(memory_space=pltpu.HBM)
    dma = lambda *shape: pltpu.SemaphoreType.DMA(shape)
    place = lambda x: pltpu.with_memory_space_constraint(x, pltpu.HBM)
    kv, attended = pl.pallas_call(
        exchange,
        name="exchange",
        out_shape=(pltpu.HBM((32, 4, 4, 2, TILE, 256), bf16), pltpu.HBM((256, 2048), bf16)),
        in_specs=[hbm] * 6,
        out_specs=(hbm, hbm),
        scratch_shapes=[
            pltpu.VMEM((4096, 128), bf16), pltpu.VMEM((4096, 128), bf16), pltpu.VMEM((4, 2, TILE, 256), bf16),
            pltpu.VMEM((1280, 256), bf16), pltpu.VMEM((1280, 256), bf16),
            pltpu.VMEM((1, 2048), i32), pltpu.VMEM((256, 1280), f32),
            pltpu.VMEM((4096, 128), f32), pltpu.VMEM((4096, 128), f32), pltpu.VMEM((4096, 128), f32),
            dma(3, 2), dma(3, 2), dma(1), dma(3, 5), dma(3, 5), dma(4, 3, 5), dma(4, 3, 5),
            dma(4, 4, 5), dma(4, 4, 5), dma(6, 2), dma(6, 2), dma(21), dma(16),
        ],
        compiler_params=pltpu.CompilerParams(collective_id=0, has_side_effects=True, vmem_limit_bytes=48 << 20),
    )(*(place(x) for x in (image_keys, image_values, self_k[0], self_v[0], doc_ids, self_q[0])))
    cross_out, self_out = pl.pallas_call(
        cross_kernel,
        name="cross_attend",
        out_shape=(pltpu.HBM((256, 2048), bf16), pltpu.HBM((256, 2048), bf16)),
        in_specs=[hbm] * 6,
        out_specs=(hbm, hbm),
        scratch_shapes=[
            pltpu.SMEM((4, 8, 32), i32), pltpu.SMEM((128,), i32), pltpu.SMEM((1, 2, 32), i32),
            pltpu.VMEM((4096, 128), bf16), pltpu.VMEM((4096, 128), bf16), pltpu.VMEM((2, 128, 2, TILE, 256), bf16), pltpu.VMEM((256, 2048), bf16),
            pltpu.VMEM((4096, 128), f32), pltpu.VMEM((4096, 128), f32), pltpu.VMEM((4096, 128), f32),
            dma(3), dma(2, 16), dma(2, 16), dma(2), dma(2, 4),
        ],
        compiler_params=pltpu.CompilerParams(vmem_limit_bytes=48 << 20),
    )(*(place(x) for x in (image_list, image_lengths, cross_mask, cross_q[0])), place(kv), place(attended))
    return self_out[None], cross_out[None]


def solution(mesh):
    in_specs = (
        P("enc", "seq", "mp"),
        P("enc", "seq", "mp"),
        P("enc", "seq", "mp"),
        P("enc", None),
        P("enc", "seq", "mp"),
        P(("seq", "enc"), "mp", None),
        P(("seq", "enc"), "mp", None),
        P(),
        P(),
        P("enc", "seq", None),
    )
    out_specs = (P("enc", "seq", "mp"), P("enc", "seq", "mp"))
    return jax.shard_map(local, mesh=mesh, in_specs=in_specs, out_specs=out_specs, check_vma=False)
```
